256 devices in a mesh: sens: 8 (over z_lo, core), pts: 32 (over y, z_hi, x).
Axes of the slice: x: 4, y: 4, z: 8 (z_hi: 2, z_lo: 4; z = z_hi * 4 + z_lo), core: 2. Of those that a mesh axis runs over, the one named last changes fastest.
Arguments:
- kernel: float32 [64, 2048, 384], P('sens', 'pts'), may hold values from -0.0068359375 to 0.0068359375
- vectors: float32 [8, 2048, 384], P(None, 'pts'), may hold values from -6 to 6
- noise_scale: float32 [64], P('sens'), may hold values from 0.5 to 2
- sensor_group: int32 [64], P('sens'), may hold values from 0 to 3
- correlation: float32 [4, 384, 384], replicated, may hold values from -0.3125 to 0.3125
- stiffness: float32 [2048], P('pts'), may hold values from 0.2 to 1
- couplings: float32 [4, 2048], P(None, 'pts'), may hold values from 0.05 to 0.5
- neighbors: int32 [4, 2048], P(None, 'pts'), may hold values from 0 to 2047, as said below
Outputs:
- hessian_action: float32 [8, 2048, 384], P('sens', 'pts')
The draws below stay inside these ranges and needn't reach their ends.
Inputs may be any that keep to these rules, and one draw needn't show every extreme that they name: `neighbors`: points are numbered row by row on a grid of rows of 16 points; every neighbor of point p lies in p's grid row or in one of the two rows beside it.
All inputs are finite; a program needn't handle non-finite values.
Results may differ from the reference program's by a relative error of at most 0.0001.
Values sent between devices are 32-bit elements; how exact they have to be, the bound alone decides.
A program may use at most 64 MiB of HBM per device.

```python
import math
import jax
import jax.numpy as jnp
from jax import lax

K = 8
NT = 384
NB = 4
S_DEV = 8
COLS = 16
S = 64
NP = 2048
N_SENS = 8


def draw_neighbors(key, part):
    grid_rows = NP // COLS
    index = jnp.arange(NP, dtype=jnp.int32)
    row = index // COLS
    column = index % COLS
    jitter = jax.random.randint(jax.random.fold_in(key, 17), (2, NP), -1, 2).astype(jnp.int32)
    upper = jnp.maximum(row - 1, 0) * COLS + jnp.clip(column + jitter[0], 0, COLS - 1)
    lower = jnp.minimum(row + 1, grid_rows - 1) * COLS + jnp.clip(column + jitter[1], 0, COLS - 1)
    left = row * COLS + jnp.maximum(column - 1, 0)
    right = row * COLS + jnp.minimum(column + 1, COLS - 1)
    return jnp.stack([upper, lower, left, right]).astype(jnp.int32)


def touch_ends(result, rng, low, top_value):
    dims = result.shape
    index_at = [jax.random.randint(jax.random.fold_in(rng, axis), (), 0, dims[axis]) for axis in range(len(dims))]
    result = result.at[tuple(index_at)].set(low)
    longest = dims.index(max(dims))
    index_at[longest] = (index_at[longest] + 1) % dims[longest]
    return result.at[tuple(index_at)].set(top_value)


def shard_levels(rng, dims, cuts, smallest, largest):
    factor_of = 1.0
    for position, shards_of in cuts:
        steps = jax.random.uniform(jax.random.fold_in(jax.random.fold_in(rng, 6), position), (shards_of,), jnp.float32, smallest / len(cuts), largest / len(cuts))
        factor_of = factor_of * jnp.repeat(jnp.exp(steps), dims[position] // shards_of).reshape((-1,) + (1,) * (len(dims) - 1 - position))
    return factor_of


def centred(own_key, dims, spread, most, cuts=(), held_as=jnp.bfloat16):
    values = spread * jax.random.normal(own_key, dims, jnp.float32)
    if cuts:
        values = values * shard_levels(own_key, dims, cuts, -0.22, 0.18)
    return jnp.clip(values, -most, most).astype(held_as)


def setup_inputs(seed: int = 0) -> dict:
    keys = jax.random.split(jax.random.key(seed), 9)
    kernel = centred(keys[0], (S, NP, NT), (NP * NT) ** -0.5, 0.0068359375, ((0, 8), (1, 32)), jnp.float32)
    vectors = centred(keys[1], (K, NP, NT), 1.0, 6.0, ((1, 32),), jnp.float32)
    noise_scale = jnp.clip(jnp.exp(math.log(2.0) - 1.3862944 * jax.random.uniform(keys[2], (S,), jnp.float32) ** shard_levels(keys[2], (S,), ((0, 8),), -0.2, 0.2)), 0.5, 2.0)
    sensor_group = touch_ends(jax.random.randint(keys[3], (S,), 0, NB), jax.random.fold_in(keys[3], 1), 0, NB - 1).astype(jnp.int32)
    correlation = centred(keys[4], (NB, NT, NT), NT ** -0.5, 0.3125, (), jnp.float32)
    stiffness = jnp.clip(jnp.exp(math.log(1.0) - 1.609438 * jax.random.uniform(keys[5], (NP,), jnp.float32) ** shard_levels(keys[5], (NP,), ((0, 32),), -0.2, 0.2)), 0.2, 1.0)
    couplings = jnp.clip(jnp.exp(math.log(0.5) - 2.3025851 * jax.random.uniform(keys[6], (4, NP), jnp.float32) ** shard_levels(keys[6], (4, NP), ((1, 32),), -0.2, 0.2)), 0.05, 0.5)
    neighbors = draw_neighbors(jax.random.fold_in(keys[8], 71), 0)
    return dict(kernel=kernel, vectors=vectors, noise_scale=noise_scale, sensor_group=sensor_group, correlation=correlation, stiffness=stiffness, couplings=couplings, neighbors=neighbors)


def reference(kernel, vectors, noise_scale, sensor_group, correlation, stiffness, couplings, neighbors):
    span = 2 * NT
    vec_hat = jnp.fft.rfft(vectors, n=span, axis=-1)
    blocks = kernel.reshape(N_SENS, S_DEV, NP, NT)

    def forward_block(block):
        kern_hat = jnp.fft.rfft(block, n=span, axis=-1)
        pred_hat = jnp.einsum('kpf,spf->ksf', vec_hat, kern_hat)
        return jnp.fft.irfft(pred_hat, n=span, axis=-1)[..., :NT]

    predicted = lax.map(forward_block, blocks)
    predicted = jnp.transpose(predicted, (1, 0, 2, 3)).reshape(K, S, NT)
    corr_sensor = correlation[sensor_group]
    mixed = jnp.einsum('sut,kst->ksu', corr_sensor, predicted, precision=lax.Precision.HIGHEST)
    residual = noise_scale[None, :, None] * (predicted + mixed)
    res_blocks = jnp.transpose(residual.reshape(K, N_SENS, S_DEV, NT), (1, 0, 2, 3))

    def adjoint(total, pair):
        block, res = pair
        kern_hat = jnp.fft.rfft(block, n=span, axis=-1)
        res_hat = jnp.fft.rfft(res, n=span, axis=-1)
        return total + jnp.einsum('ksf,spf->kpf', res_hat, jnp.conj(kern_hat)), None

    start = jnp.zeros(vec_hat.shape, vec_hat.dtype)
    grad_hat, _ = lax.scan(adjoint, start, (blocks, res_blocks))
    data_term = jnp.fft.irfft(grad_hat, n=span, axis=-1)[..., :NT]
    gathered = vectors[:, neighbors]
    prior_term = stiffness[None, :, None] * vectors
    prior_term = prior_term + jnp.sum(couplings[None, :, :, None] * (vectors[:, None] - gathered), axis=1)
    return data_term + prior_term
```

```python
import functools
import math

import jax
import jax.numpy as jnp
import numpy as np
from jax import lax
from jax.experimental import pallas as pl
from jax.experimental.pallas import tpu as pltpu
from jax.sharding import PartitionSpec as P

F32, BF16 = jnp.float32, jnp.bfloat16
K, NT, NB, SD, PD, COLS = 8, 384, 4, 8, 64, 16
F2 = 2 * NT
LANES = 128
FT = NT // LANES
PLANE = sorted(
    ((dx, dy) for dx in range(4) for dy in range(4) if dx or dy),
    key=lambda d: -(min(d[0], 4 - d[0]) + min(d[1], 4 - d[1])),
)


def table():
    t = np.arange(NT)
    angle = 2.0 * math.pi / F2 * (t[:, None] * t[None, :] % F2)
    second = -np.sin(angle)
    second[:, 0] = np.where(t % 2 == 0, 1.0, -1.0)
    full = np.concatenate([np.cos(angle), second], axis=1).astype(np.float32)
    high = full.astype(BF16)
    low = (full - high.astype(np.float32)).astype(BF16)
    return high, low


def split(x):
    high = x.astype(BF16)
    low = (x - high.astype(F32)).astype(BF16)
    return high, low


def stack(x):
    high, low = split(x)
    return jnp.concatenate([high, low, high], axis=1)


def matmul(a, b):
    return lax.dot_general(a, b, (((1,), (0,)), ((), ())), preferred_element_type=F32)


def matmul_t(a, b):
    return lax.dot_general(a, b, (((1,), (1,)), ((), ())), preferred_element_type=F32)


def body(
    kern_hbm, vec_hbm, noise, group, corr_hbm, stiff_hbm, coup_hbm, nbr_hbm, fh_hbm, fl_hbm,
    out_ref,
    kern, vec, corr, stiff, coup, nbr, fh, fl,
    kh, km, vh, ph, part, rs_in, zsum, z_in, mine, resid, rh, grad, prior,
    halo_lo, halo_hi, core_out, core_in, line_out, line_in,
    load_sem, halo_send, halo_recv, rs_send, rs_recv, z_send, z_recv, ag_send, ag_recv,
    core_send, core_recv, line_send, line_recv,
):
    pts, sens = lax.axis_index("pts"), lax.axis_index("sens")
    x, zh, y = pts % 4, pts // 4 % 2, pts // 8
    zl, core = sens // 2, sens % 2

    def plane(dx, dy):
        tx, ty = (x + dx) % 4, (y + dy) % 4
        return ty * 4 + tx, (ty * 2 + zh) * 4 + tx

    own_chunk = y * 4 + x
    z_peer = (y * 2 + 1 - zh) * 4 + x
    up, down = (pts + 1) % 32, (pts + 31) % 32
    core_peer = zl * 2 + 1 - core
    line = [3 - zl, (zl + 2) % 4, zl + 1 - 2 * (zl % 2), zl]

    loads = [
        pltpu.make_async_copy(src, dst, load_sem.at[i])
        for i, (src, dst) in enumerate(
            [
                (kern_hbm, kern), (fh_hbm, fh), (fl_hbm, fl), (vec_hbm, vec), (corr_hbm, corr),
                (stiff_hbm, stiff), (coup_hbm, coup), (nbr_hbm, nbr),
            ]
        )
    ]
    for copy in loads:
        copy.start()

    barrier = pltpu.get_barrier_semaphore()
    greet = [{"pts": plane(dx, dy)[1]} for dx, dy in PLANE]
    greet += [{"pts": z_peer}, {"pts": up}, {"pts": down}, {"sens": core_peer}]
    greet += [{"sens": line[i] * 2 + core} for i in range(3)]
    for target in greet:
        pl.semaphore_signal(barrier, inc=1, device_id=target, device_id_type=pl.DeviceIdType.MESH)

    def remote(src, dst, send, recv, target):
        return pltpu.make_async_remote_copy(
            src_ref=src, dst_ref=dst, send_sem=send, recv_sem=recv,
            device_id=target, device_id_type=pl.DeviceIdType.MESH,
        )

    freq = lax.broadcasted_iota(jnp.int32, (1, F2), 1)
    weight = jnp.where(freq % NT == 0, 1.0 / F2, 2.0 / F2).astype(F32)

    for i in range(3):
        loads[i].wait()
    forward = jnp.concatenate([fh[...], fh[...], fl[...]], axis=0)

    @pl.loop(0, 2)
    def _(i):
        rows = kern[pl.ds(i * 4, 4)].reshape(4 * PD, NT)
        hat = matmul(stack(rows), forward) * weight
        kh[pl.ds(i * 4, 4)] = hat.reshape(4, PD, F2)
        km[pl.ds(i * 4, 4)] = (hat[:, :NT] - hat[:, NT:]).reshape(4, PD, NT)

    loads[3].wait()

    @pl.loop(0, 2)
    def _(i):
        rows = vec[pl.ds(i * 4, 4)].reshape(4 * PD, NT)
        vh[pl.ds(i * 4, 4)] = matmul(stack(rows), forward).reshape(4, PD, F2)

    lane = lax.broadcasted_iota(jnp.int32, (8, LANES), 1)

    @pl.loop(0, FT * (SD // 2))
    def _(it):
        ft, s0 = it // (SD // 2), it % (SD // 2) * 2
        re = pl.ds(pl.multiple_of(ft * LANES, LANES), LANES)
        im = pl.ds(pl.multiple_of(NT + ft * LANES, LANES), LANES)
        keep = lane + ft * LANES > 0
        acc = [[None] * K for _ in range(6)]
        for p in range(PD // 8):
            rows = pl.ds(p * 8, 8)
            right = []
            for j in range(2):
                c, d = kh[s0 + j, rows, re], kh[s0 + j, rows, im]
                right.append((c, d, c + d))
            for k in range(K):
                a, b = vh[k, rows, re], vh[k, rows, im]
                left = (a, b, a + b)
                for j in range(2):
                    for q in range(3):
                        term = left[q] * right[j][q]
                        old = acc[j * 3 + q][k]
                        acc[j * 3 + q][k] = term if old is None else old + term
        for j in range(2):
            p1, p2, p3 = (
                jnp.concatenate([jnp.sum(v, axis=0, keepdims=True) for v in acc[j * 3 + q]], axis=0)
                for q in range(3)
            )
            rows = pl.ds(pl.multiple_of((s0 + j) * 8, 8), 8)
            ph[rows, re] = jnp.where(keep, p1 - p2, p1)
            ph[rows, im] = jnp.where(keep, p3 - p1 - p2, p2)

    inverse = jnp.concatenate([fh[...], fh[...], fl[...]], axis=1)
    pred = matmul_t(stack(ph[...]), inverse)
    for c in range(16):
        part[c] = pred[c * 4 : c * 4 + 4]

    pl.semaphore_wait(barrier, len(greet))

    rs = []
    for i, (dx, dy) in enumerate(PLANE):
        chunk, target = plane(dx, dy)
        rs.append(remote(part.at[chunk], rs_in.at[i], rs_send.at[i], rs_recv.at[i], {"pts": target}))
        rs[-1].start()
    halo = [
        remote(vec.at[sens, pl.ds(PD - COLS, COLS)], halo_lo, halo_send.at[0], halo_recv.at[0], {"pts": up}),
        remote(vec.at[sens, pl.ds(0, COLS)], halo_hi, halo_send.at[1], halo_recv.at[1], {"pts": down}),
    ]
    for copy in halo:
        copy.start()

    loads[4].wait()
    sensor = own_chunk // 2
    scale = noise[sensor]
    mix_high, mix_low = split(corr[group[sensor]])
    mix = jnp.concatenate([mix_high, mix_high, mix_low], axis=1)

    total = part[own_chunk]
    for i in range(len(PLANE) - 1, -1, -1):
        rs[i].wait_recv()
        total = total + rs_in[i]
    zsum[...] = total
    swap = remote(zsum, z_in, z_send, z_recv, {"pts": z_peer})
    swap.start()

    for i in range(5, 8):
        loads[i].wait()
    for copy in halo:
        copy.wait_recv()
    q = lax.broadcasted_iota(jnp.int32, (PD + 2 * COLS, PD), 0)
    here = lax.broadcasted_iota(jnp.int32, (PD + 2 * COLS, PD), 1) + COLS
    local = nbr[...] - pts * PD + COLS
    links = coup[...]
    diagonal = stiff[...] + jnp.sum(links, axis=0, keepdims=True)
    pick = jnp.where(q == here, diagonal, 0.0)
    for j in range(4):
        pick = pick - jnp.where(q == local[j : j + 1], links[j : j + 1], 0.0)
    padded = jnp.concatenate([halo_lo[...], vec[sens], halo_hi[...]], axis=0)
    prior[...] = lax.dot_general(
        pick, padded, (((0,), (0,)), ((), ())),
        precision=lax.Precision.HIGHEST, preferred_element_type=F32,
    )

    swap.wait_recv()
    total = zsum[...] + z_in[...]
    tall = jnp.concatenate([total, jnp.zeros((12, NT), F32)], axis=0)
    mixed = matmul_t(stack(tall), mix)[:4]
    value = scale * (total + mixed)
    mine[...] = value
    resid[own_chunk] = value
    ag = []
    for i, (dx, dy) in enumerate(PLANE):
        _, target = plane(dx, dy)
        ag.append(remote(mine, resid.at[own_chunk], ag_send.at[i], ag_recv.at[i], {"pts": target}))
        ag[-1].start()
    for i, (dx, dy) in enumerate(PLANE):
        source = plane(-dx, -dy)[0]
        remote(mine, resid.at[source], ag_send.at[i], ag_recv.at[i], {"pts": up}).wait_recv()

    rows = jnp.concatenate([resid[c] for c in range(16)], axis=0)
    hat = matmul(stack(rows), forward)
    for c in range(2 * FT):
        rh[c] = hat[:, c * LANES : (c + 1) * LANES]

    core_copies, line_copies = [], []
    for i in range(4):
        first = line[i] * 2 + 1 - core
        second = line[i] * 2 + core

        @pl.loop(0, 2 * FT)
        def _(it, first=first, second=second):
            ft, which = it // 2, it % 2
            k = first + which * (second - first)
            re = pl.ds(pl.multiple_of(ft * LANES, LANES), LANES)
            im = pl.ds(pl.multiple_of(NT + ft * LANES, LANES), LANES)
            keep = lane + ft * LANES > 0
            left = []
            for s in range(SD):
                a = rh[ft, pl.ds(s * 8 + k, 8, stride=0), :]
                b = rh[FT + ft, pl.ds(s * 8 + k, 8, stride=0), :]
                left.append((a, b, a + b))
            for p in range(PD // 8):
                rows = pl.ds(p * 8, 8)
                p1 = p2 = p3 = None
                for s in range(SD):
                    t1 = left[s][0] * kh[s, rows, re]
                    t2 = left[s][1] * kh[s, rows, im]
                    t3 = left[s][2] * km[s, rows, re]
                    p1, p2, p3 = (t1, t2, t3) if s == 0 else (p1 + t1, p2 + t2, p3 + t3)
                here = pl.ds(pl.multiple_of(which * PD + p * 8, 8), 8)
                grad[here, re] = jnp.where(keep, p1 + p2, p1)
                grad[here, im] = jnp.where(keep, p3 - p1 + p2, p2)

        data = matmul_t(stack(grad[...]), inverse)
        core_out[i] = data[:PD]
        copy = remote(core_out.at[i], core_in.at[i], core_send.at[i], core_recv.at[i], {"sens": core_peer})
        copy.start()
        core_copies.append(copy)
        line_out[i] = data[PD:]
        if i:
            finish(i - 1, core_copies, core_in, line_out)
            copy = remote(
                line_out.at[i - 1], line_in.at[i - 1], line_send.at[i - 1], line_recv.at[i - 1],
                {"sens": line[i - 1] * 2 + core},
            )
            copy.start()
            line_copies.append(copy)
    finish(3, core_copies, core_in, line_out)
    result = line_out[3] + prior[...]
    for i in (2, 1, 0):
        line_copies[i].wait_recv()
        result = result + line_in[i]
    out_ref[0] = result

    for copy in halo + rs + [swap] + ag + core_copies + line_copies:
        copy.wait_send()


def finish(i, core_copies, core_in, line_out):
    core_copies[i].wait_recv()
    line_out[i] = line_out[i] + core_in[i]


def local(kernel, vectors, noise_scale, sensor_group, correlation, stiffness, couplings, neighbors):
    high, low = table()
    anywhere = pl.BlockSpec(memory_space=pl.ANY)
    smem = pl.BlockSpec(memory_space=pltpu.SMEM)
    dma = pltpu.SemaphoreType.DMA
    count = len(PLANE)
    return pl.pallas_call(
        body,
        out_shape=jax.ShapeDtypeStruct((1, PD, NT), F32),
        in_specs=[anywhere, anywhere, smem, smem] + [anywhere] * 6,
        out_specs=pl.BlockSpec(memory_space=pltpu.VMEM),
        scratch_shapes=[
            pltpu.VMEM((SD, PD, NT), F32),
            pltpu.VMEM((K, PD, NT), F32),
            pltpu.VMEM((NB, NT, NT), F32),
            pltpu.VMEM((1, PD), F32),
            pltpu.VMEM((4, PD), F32),
            pltpu.VMEM((4, PD), jnp.int32),
            pltpu.VMEM((NT, F2), BF16),
            pltpu.VMEM((NT, F2), BF16),
            pltpu.VMEM((SD, PD, F2), F32),
            pltpu.VMEM((SD, PD, NT), F32),
            pltpu.VMEM((K, PD, F2), F32),
            pltpu.VMEM((SD * K, F2), F32),
            pltpu.VMEM((16, 4, NT), F32),
            pltpu.VMEM((count, 4, NT), F32),
            pltpu.VMEM((4, NT), F32),
            pltpu.VMEM((4, NT), F32),
            pltpu.VMEM((4, NT), F32),
            pltpu.VMEM((16, 4, NT), F32),
            pltpu.VMEM((2 * FT, SD * K, LANES), F32),
            pltpu.VMEM((2 * PD, F2), F32),
            pltpu.VMEM((PD, NT), F32),
            pltpu.VMEM((COLS, NT), F32),
            pltpu.VMEM((COLS, NT), F32),
            pltpu.VMEM((4, PD, NT), F32),
            pltpu.VMEM((4, PD, NT), F32),
            pltpu.VMEM((4, PD, NT), F32),
            pltpu.VMEM((3, PD, NT), F32),
            dma((8,)),
            dma((2,)), dma((2,)),
            dma((count,)), dma((count,)),
            dma, dma,
            dma((count,)), dma((count,)),
            dma((4,)), dma((4,)),
            dma((3,)), dma((3,)),
        ],
        compiler_params=pltpu.CompilerParams(collective_id=0, has_side_effects=True),
    )(
        kernel, vectors, noise_scale, sensor_group, correlation, stiffness.reshape(1, PD),
        couplings, neighbors, jnp.asarray(high), jnp.asarray(low),
    )


def solution(mesh):
    in_specs = (
        P("sens", "pts", None),
        P(None, "pts", None),
        P("sens"),
        P("sens"),
        P(),
        P("pts"),
        P(None, "pts"),
        P(None, "pts"),
    )
    return jax.shard_map(
        local, mesh=mesh, in_specs=in_specs, out_specs=P("sens", "pts", None), check_vma=False
    )
```

```python
import contextlib
import math

import jax
import jax.numpy as jnp
import numpy as np
from jax import lax
from jax.experimental import pallas as pl
from jax.experimental.pallas import tpu as pltpu
from jax.sharding import PartitionSpec as P

F32, BF16 = jnp.float32, jnp.bfloat16
phase = lambda name: contextlib.nullcontext()
K, NT, NB, SD, PD, COLS = 8, 384, 4, 8, 64, 16
F2 = 2 * NT
LANES = 128
FT = NT // LANES
VECTORS = (0, 2, 4, 6, 1, 3, 5, 7)
SUB = 2
PLANE = sorted(
    ((dx, dy) for dx in range(4) for dy in range(4) if dx or dy),
    key=lambda d: -(min(d[0], 4 - d[0]) + min(d[1], 4 - d[1])),
)


def table():
    t = np.arange(NT)
    angle = 2.0 * math.pi / F2 * (t[:, None] * t[None, :] % F2)
    second = -np.sin(angle)
    second[:, 0] = np.where(t % 2 == 0, 1.0, -1.0)
    full = np.concatenate([np.cos(angle), second], axis=1).astype(np.float32)
    high = full.astype(BF16)
    low = (full - high.astype(np.float32)).astype(BF16)
    return high, low


def split(x):
    high = x.astype(BF16)
    low = (x - high.astype(F32)).astype(BF16)
    return high, low


def stack(x):
    high, low = split(x)
    return jnp.concatenate([high, low, high], axis=1)


def matmul(a, b):
    return lax.dot_general(a, b, (((1,), (0,)), ((), ())), preferred_element_type=F32)


def matmul_t(a, b):
    return lax.dot_general(a, b, (((1,), (1,)), ((), ())), preferred_element_type=F32)


def body(
    kern_hbm, vec_hbm, noise, group, corr_hbm, stiff_hbm, coup_hbm, nbr_hbm, fh_hbm, fl_hbm,
    out_ref,
    kern, vec, corr, stiff, coup, nbr, fh, fl,
    kh, km, vh, ph, part, rs_in, zsum, z_in, mine, resid, rh, grad, prior,
    halo_lo, halo_hi, line_out, line_in,
    load_sem, halo_send, halo_recv, rs_send, rs_recv, z_send, z_recv, ag_send, ag_recv,
    share_send, share_recv, line_send, line_recv,
):
    pts, sens = lax.axis_index("pts"), lax.axis_index("sens")
    x, zh, y = pts % 4, pts // 4 % 2, pts // 8
    zl, core = sens // 2, sens % 2

    def plane(dx, dy):
        tx, ty = (x + dx) % 4, (y + dy) % 4
        return ty * 4 + tx, (ty * 2 + zh) * 4 + tx

    own_chunk = y * 4 + x
    z_peer = (y * 2 + 1 - zh) * 4 + x
    up, down = (pts + 1) % 32, (pts + 31) % 32
    core_peer = zl * 2 + 1 - core
    half = x % 2
    order = [3 - zl, (12 - 2 * zl) % 5, 3 - (12 - 2 * zl) % 5, zl]
    heads = [1 + zl % 2, order[1], order[2]]
    inner = zl * (3 - zl) // 2

    loads = [
        pltpu.make_async_copy(src, dst, load_sem.at[i])
        for i, (src, dst) in enumerate(
            [
                (kern_hbm, kern), (fh_hbm, fh), (fl_hbm, fl), (vec_hbm, vec), (corr_hbm, corr),
                (stiff_hbm, stiff), (coup_hbm, coup), (nbr_hbm, nbr),
            ]
        )
    ]
    for copy in loads:
        copy.start()

    barrier = pltpu.get_barrier_semaphore()
    greet = [{"pts": plane(dx, dy)[1]} for dx, dy in PLANE]
    greet += [{"pts": plane(dx, dy)[1], "sens": core_peer} for dx, dy in PLANE]
    greet += [{"pts": z_peer}, {"pts": up}, {"pts": down}, {"sens": core_peer}]
    greet += [{"sens": (zl + i) % 4 * 2 + core} for i in range(1, 4)]
    for target in greet:
        pl.semaphore_signal(barrier, inc=1, device_id=target, device_id_type=pl.DeviceIdType.MESH)

    def remote(src, dst, send, recv, target):
        return pltpu.make_async_remote_copy(
            src_ref=src, dst_ref=dst, send_sem=send, recv_sem=recv,
            device_id=target, device_id_type=pl.DeviceIdType.MESH,
        )

    freq = lax.broadcasted_iota(jnp.int32, (1, F2), 1)
    weight = jnp.where(freq % NT == 0, 1.0 / F2, 2.0 / F2).astype(F32)

    with phase("p_load"):
        for i in range(3):
            loads[i].wait()
    forward = jnp.concatenate([fh[...], fh[...], fl[...]], axis=0)

    with phase("p_kdft"):
        @pl.loop(0, 2)
        def _(i):
            rows = kern[pl.ds(i * 4, 4)].reshape(4 * PD, NT)
            hat = matmul(stack(rows), forward) * weight
            kh[pl.ds(i * 4, 4)] = hat.reshape(4, PD, F2)
            km[pl.ds(i * 4, 4)] = (hat[:, :NT] - hat[:, NT:]).reshape(4, PD, NT)

    loads[3].wait()

    with phase("p_vdft"):
        @pl.loop(0, 2)
        def _(i):
            rows = vec[pl.ds(i * 4, 4)].reshape(4 * PD, NT)
            vh[pl.ds(i * 4, 4)] = matmul(stack(rows), forward).reshape(4, PD, F2)

    lane = lax.broadcasted_iota(jnp.int32, (8, LANES), 1)

    with phase("p_spec"):
        @pl.loop(0, FT * (SD // 2))
        def _(it):
            ft, s0 = it // (SD // 2), it % (SD // 2) * 2
            re = pl.ds(pl.multiple_of(ft * LANES, LANES), LANES)
            im = pl.ds(pl.multiple_of(NT + ft * LANES, LANES), LANES)
            keep = lane + ft * LANES > 0
            acc = [[None] * K for _ in range(6)]
            for p in range(PD // 8):
                rows = pl.ds(p * 8, 8)
                right = []
                for j in range(2):
                    c, d = kh[s0 + j, rows, re], kh[s0 + j, rows, im]
                    right.append((c, d, c + d))
                for k in range(K):
                    a, b = vh[VECTORS[k], rows, re], vh[VECTORS[k], rows, im]
                    left = (a, b, a + b)
                    for j in range(2):
                        for q in range(3):
                            term = left[q] * right[j][q]
                            old = acc[j * 3 + q][k]
                            acc[j * 3 + q][k] = term if old is None else old + term
            for j in range(2):
                p1, p2, p3 = (
                    jnp.concatenate([jnp.sum(v, axis=0, keepdims=True) for v in acc[j * 3 + q]], axis=0)
                    for q in range(3)
                )
                rows = pl.ds(pl.multiple_of((s0 + j) * 8, 8), 8)
                ph[rows, re] = jnp.where(keep, p1 - p2, p1)
                ph[rows, im] = jnp.where(keep, p3 - p1 - p2, p2)

    inverse = jnp.concatenate([fh[...], fh[...], fl[...]], axis=1)
    with phase("p_inv"):
        pred = matmul_t(stack(ph[...]), inverse)
        for c in range(16):
            part[c] = pred[c * 4 : c * 4 + 4]

    with phase("p_bar"):
        pl.semaphore_wait(barrier, len(greet))

    rs = []
    for i, (dx, dy) in enumerate(PLANE):
        chunk, target = plane(dx, dy)
        rs.append(remote(part.at[chunk], rs_in.at[i], rs_send.at[i], rs_recv.at[i], {"pts": target}))
        rs[-1].start()
    halo = [
        remote(vec.at[sens, pl.ds(PD - COLS, COLS)], halo_lo, halo_send.at[0], halo_recv.at[0], {"pts": up}),
        remote(vec.at[sens, pl.ds(0, COLS)], halo_hi, halo_send.at[1], halo_recv.at[1], {"pts": down}),
    ]
    share = remote(kh.at[pl.ds(0, SD)], kh.at[pl.ds(SD, SD)], share_send, share_recv, {"sens": core_peer})
    for copy in halo + [share]:
        copy.start()

    loads[4].wait()
    sensor = own_chunk // 2
    scale = noise[sensor]
    mix_high, mix_low = split(corr[group[sensor]])
    mix = jnp.concatenate([mix_high, mix_high, mix_low], axis=1)

    with phase("p_prior"):
        for i in range(5, 8):
            loads[i].wait()
        for copy in halo:
            copy.wait_recv()
        q = lax.broadcasted_iota(jnp.int32, (PD + 2 * COLS, PD), 0)
        here = lax.broadcasted_iota(jnp.int32, (PD + 2 * COLS, PD), 1) + COLS
        local = nbr[...] - pts * PD + COLS
        links = coup[...]
        diagonal = stiff[...] + jnp.sum(links, axis=0, keepdims=True)
        pick = jnp.where(q == here, diagonal, 0.0)
        for j in range(4):
            pick = pick - jnp.where(q == local[j : j + 1], links[j : j + 1], 0.0)
        padded = jnp.concatenate([halo_lo[...], vec[sens], halo_hi[...]], axis=0)
        prior[...] = lax.dot_general(
            pick, padded, (((0,), (0,)), ((), ())),
            precision=lax.Precision.HIGHEST, preferred_element_type=F32,
        )

    total = part[own_chunk]
    with phase("p_rswait"):
        for i in range(len(PLANE) - 1, -1, -1):
            rs[i].wait_recv()
            total = total + rs_in[i]
    zsum[...] = total
    swap = remote(zsum, z_in, z_send, z_recv, {"pts": z_peer})
    swap.start()

    with phase("p_zwait"):
        swap.wait_recv()
    total = zsum[...] + z_in[...]
    tall = jnp.concatenate([total, jnp.zeros((12, NT), F32)], axis=0)
    mixed = matmul_t(stack(tall), mix)[:4]
    value = scale * (total + mixed)
    mine[...] = value
    slot = sensor + SD * ((half + core) % 2)
    home = resid.at[slot]
    ag = []
    for i, (dx, dy) in enumerate(PLANE):
        target = {"pts": plane(dx, dy)[1], "sens": zl * 2 + half}
        ag.append(remote(mine, home, ag_send.at[i], ag_recv.at[slot], target))
        ag[-1].start()
    beside = remote(mine, home, ag_send.at[len(PLANE)], ag_recv.at[slot], {"sens": core_peer})

    @pl.when(half == core)
    def _():
        resid[slot] = value

    @pl.when(half != core)
    def _():
        beside.start()

    with phase("p_share"):
        share.wait_recv()
        for s in range(SD, 2 * SD):
            km[s] = kh[s, :, :NT] - kh[s, :, NT:]

    with phase("p_agwait"):
        for i in range(2 * SD):

            @pl.when((half + core) % 2 * 2 * SD + (slot - i) * (slot - i) > 0)
            def _(i=i):
                remote(mine, resid.at[i], ag_send.at[0], ag_recv.at[i], {"sens": core_peer}).wait_recv()

    with phase("p_rdft"):
        rows = jnp.concatenate([resid[c] for c in range(2 * SD)], axis=0)
        hat = matmul(stack(rows), forward)
        for c in range(2 * FT):
            rh[c] = hat[:, c * LANES : (c + 1) * LANES]

    rows_sub = PD // SUB

    def line_copy(i, j):
        piece = pl.ds(j * rows_sub, rows_sub)
        seat = 3 * (1 - inner) if i == 0 else i
        return remote(
            line_out.at[i, piece], line_in.at[seat, piece], line_send.at[i, j], line_recv.at[seat, j],
            {"sens": heads[i] * 2 + core},
        )

    def line_arrival(i, j):
        piece = pl.ds(j * rows_sub, rows_sub)
        return remote(
            line_out.at[0, piece], line_in.at[i, piece], line_send.at[0, j], line_recv.at[i, j],
            {"sens": core_peer},
        )

    for i in range(4):
        v = order[i]

        with phase("p_adj%d" % i):

            @pl.loop(0, FT)
            def _(ft, v=v):
                re = pl.ds(pl.multiple_of(ft * LANES, LANES), LANES)
                im = pl.ds(pl.multiple_of(NT + ft * LANES, LANES), LANES)
                keep = lane + ft * LANES > 0
                acc = [None] * (PD // 8)
                for s in range(2 * SD):
                    a = rh[ft, pl.ds(s * 4 + v, 8, stride=0), :]
                    b = rh[FT + ft, pl.ds(s * 4 + v, 8, stride=0), :]
                    ab = a + b
                    for p in range(PD // 8):
                        rows = pl.ds(p * 8, 8)
                        terms = (a * kh[s, rows, re], b * kh[s, rows, im], ab * km[s, rows, re])
                        acc[p] = terms if s == 0 else tuple(m + n for m, n in zip(acc[p], terms, strict=True))
                for p in range(PD // 8):
                    p1, p2, p3 = acc[p]
                    grad[pl.ds(p * 8, 8), re] = jnp.where(keep, p1 + p2, p1)
                    grad[pl.ds(p * 8, 8), im] = jnp.where(keep, p3 - p1 + p2, p2)

        with phase("p_ainv%d" % i):
            line_out[i] = matmul_t(stack(grad[...]), inverse)
        if i < 2:
            for j in range(SUB):
                line_copy(i, j).start()
        if i == 2:

            @pl.when(inner == 0)
            def _():
                for j in range(SUB):
                    line_copy(2, j).start()

    with phase("p_relay"):

        @pl.when(inner == 1)
        def _():
            for j in range(SUB):
                line_arrival(3, j).wait_recv()
                piece = pl.ds(j * rows_sub, rows_sub)
                line_out[2, piece] = line_out[2, piece] + line_in[3, piece]
                line_copy(2, j).start()

    prior[...] = prior[...] + line_out[3]

    with phase("p_linewait"):

        @pl.when(inner == 1)
        def _():
            for j in range(SUB):
                line_arrival(0, j).wait_recv()
            prior[...] = prior[...] + line_in[0]

        for i in (1, 2):
            for j in range(SUB):
                line_arrival(i, j).wait_recv()
        out_ref[0] = prior[...] + line_in[1] + line_in[2]

    with phase("p_sends"):
        for copy in halo + rs + [swap, share] + ag + [line_copy(i, j) for i in range(3) for j in range(SUB)]:
            copy.wait_send()

        @pl.when(half != core)
        def _():
            beside.wait_send()


def local(kernel, vectors, noise_scale, sensor_group, correlation, stiffness, couplings, neighbors):
    high, low = table()
    anywhere = pl.BlockSpec(memory_space=pl.ANY)
    smem = pl.BlockSpec(memory_space=pltpu.SMEM)
    dma = pltpu.SemaphoreType.DMA
    count = len(PLANE)
    return pl.pallas_call(
        body,
        out_shape=jax.ShapeDtypeStruct((1, PD, NT), F32),
        in_specs=[anywhere, anywhere, smem, smem] + [anywhere] * 6,
        out_specs=pl.BlockSpec(memory_space=pltpu.VMEM),
        scratch_shapes=[
            pltpu.VMEM((SD, PD, NT), F32),
            pltpu.VMEM((K, PD, NT), F32),
            pltpu.VMEM((NB, NT, NT), F32),
            pltpu.VMEM((1, PD), F32),
            pltpu.VMEM((4, PD), F32),
            pltpu.VMEM((4, PD), jnp.int32),
            pltpu.VMEM((NT, F2), BF16),
            pltpu.VMEM((NT, F2), BF16),
            pltpu.VMEM((2 * SD, PD, F2), F32),
            pltpu.VMEM((2 * SD, PD, NT), F32),
            pltpu.VMEM((K, PD, F2), F32),
            pltpu.VMEM((SD * K, F2), F32),
            pltpu.VMEM((16, 4, NT), F32),
            pltpu.VMEM((count, 4, NT), F32),
            pltpu.VMEM((4, NT), F32),
            pltpu.VMEM((4, NT), F32),
            pltpu.VMEM((4, NT), F32),
            pltpu.VMEM((16, 4, NT), F32),
            pltpu.VMEM((2 * FT, SD * K, LANES), F32),
            pltpu.VMEM((PD, F2), F32),
            pltpu.VMEM((PD, NT), F32),
            pltpu.VMEM((COLS, NT), F32),
            pltpu.VMEM((COLS, NT), F32),
            pltpu.VMEM((4, PD, NT), F32),
            pltpu.VMEM((4, PD, NT), F32),
            dma((8,)),
            dma((2,)), dma((2,)),
            dma((count,)), dma((count,)),
            dma, dma,
            dma((count + 1,)), dma((2 * SD,)),
            dma, dma,
            dma((3, SUB)), dma((4, SUB)),
        ],
        compiler_params=pltpu.CompilerParams(collective_id=0, has_side_effects=True),
    )(
        kernel, vectors, noise_scale, sensor_group, correlation, stiffness.reshape(1, PD),
        couplings, neighbors, jnp.asarray(high), jnp.asarray(low),
    )


def solution(mesh):
    in_specs = (
        P("sens", "pts", None),
        P(None, "pts", None),
        P("sens"),
        P("sens"),
        P(),
        P("pts"),
        P(None, "pts"),
        P(None, "pts"),
    )
    return jax.shard_map(
        local, mesh=mesh, in_specs=in_specs, out_specs=P("sens", "pts", None), check_vma=False
    )
```

```python
import contextlib
import math

import jax
import jax.numpy as jnp
import numpy as np
from jax import lax
from jax.experimental import pallas as pl
from jax.experimental.pallas import tpu as pltpu
from jax.sharding import PartitionSpec as P

F32, BF16 = jnp.float32, jnp.bfloat16
phase = lambda name: contextlib.nullcontext()
K, NT, NB, SD, PD, COLS = 8, 384, 4, 8, 64, 16
F2 = 2 * NT
LANES = 128
FT = NT // LANES
VECTORS = (0, 2, 4, 6, 1, 3, 5, 7)
SUB = 2
PLANE = sorted(
    ((dx, dy) for dx in range(4) for dy in range(4) if dx or dy),
    key=lambda d: -(min(d[0], 4 - d[0]) + min(d[1], 4 - d[1])),
)


def table():
    t = np.arange(NT)
    angle = 2.0 * math.pi / F2 * (t[:, None] * t[None, :] % F2)
    second = -np.sin(angle)
    second[:, 0] = np.where(t % 2 == 0, 1.0, -1.0)
    parts = [np.cos(angle).reshape(NT, FT, 1, LANES), second.reshape(NT, FT, 1, LANES)]
    full = np.concatenate(parts, axis=2).reshape(NT, F2).astype(np.float32)
    high = full.astype(BF16)
    low = (full - high.astype(np.float32)).astype(BF16)
    return high, low


def split(x):
    high = x.astype(BF16)
    low = (x - high.astype(F32)).astype(BF16)
    return high, low


def stack(x):
    high, low = split(x)
    return jnp.concatenate([high, low, high], axis=1)


def matmul(a, b):
    return lax.dot_general(a, b, (((1,), (0,)), ((), ())), preferred_element_type=F32)


def matmul_t(a, b):
    return lax.dot_general(a, b, (((1,), (1,)), ((), ())), preferred_element_type=F32)


def body(
    kern_hbm, vec_hbm, noise_hbm, group_hbm, corr_hbm, stiff_hbm, coup_hbm, nbr_hbm, fh_hbm, fl_hbm,
    out_ref,
    kern, vec, corr, stiff, coup, nbr, fh, fl, noise, group, lhs,
    kh, km, vh, ph, part, rs_in, zsum, z_in, mine, resid, rh, grad_a, grad_b, prior,
    halo_lo, halo_hi, line_out, line_in,
    load_sem, halo_send, halo_recv, rs_send, rs_recv, z_send, z_recv, ag_send, ag_recv,
    share_send, share_recv, line_send, line_recv,
):
    pts, sens = lax.axis_index("pts"), lax.axis_index("sens")
    x, zh, y = pts % 4, pts // 4 % 2, pts // 8
    zl, core = sens // 2, sens % 2

    def plane(dx, dy):
        tx, ty = (x + dx) % 4, (y + dy) % 4
        return ty * 4 + tx, (ty * 2 + zh) * 4 + tx

    own_chunk = y * 4 + x
    z_peer = (y * 2 + 1 - zh) * 4 + x
    up, down = (pts + 1) % 32, (pts + 31) % 32
    core_peer = zl * 2 + 1 - core
    grads = (grad_a, grad_b)
    half = x % 2
    order = [3 - zl, (12 - 2 * zl) % 5, 3 - (12 - 2 * zl) % 5, zl]
    heads = [1 + zl % 2, order[1], order[2]]
    inner = zl * (3 - zl) // 2

    loads = [
        pltpu.make_async_copy(src, dst, load_sem.at[i])
        for i, (src, dst) in enumerate(
            [
                (kern_hbm, kern), (fh_hbm, fh), (fl_hbm, fl), (vec_hbm, vec), (corr_hbm, corr),
                (stiff_hbm, stiff), (coup_hbm, coup), (nbr_hbm, nbr), (noise_hbm, noise), (group_hbm, group),
            ]
        )
    ]
    for copy in loads:
        copy.start()

    barrier = pltpu.get_barrier_semaphore()
    greet = [{"pts": plane(dx, dy)[1]} for dx, dy in PLANE]
    greet += [{"pts": plane(dx, dy)[1], "sens": core_peer} for dx, dy in PLANE]
    greet += [{"pts": z_peer}, {"pts": up}, {"pts": down}, {"sens": core_peer}]
    greet += [{"sens": (zl + i) % 4 * 2 + core} for i in range(1, 4)]
    for target in greet:
        pl.semaphore_signal(barrier, inc=1, device_id=target, device_id_type=pl.DeviceIdType.MESH)

    def remote(src, dst, send, recv, target):
        return pltpu.make_async_remote_copy(
            src_ref=src, dst_ref=dst, send_sem=send, recv_sem=recv,
            device_id=target, device_id_type=pl.DeviceIdType.MESH,
        )

    freq = lax.broadcasted_iota(jnp.int32, (1, F2), 1)
    weight = jnp.where(freq * (freq - LANES) == 0, 1.0 / F2, 2.0 / F2).astype(F32)

    lane = lax.broadcasted_iota(jnp.int32, (8, LANES), 1)

    def columns(ft):
        return slice(ft * 2 * LANES, (ft + 1) * 2 * LANES)

    def parts(ft):
        return slice(ft * 2 * LANES, ft * 2 * LANES + LANES), slice(ft * 2 * LANES + LANES, (ft + 1) * 2 * LANES)

    def keep(ft, v, other):
        return jnp.where(lane > 0, v, other) if ft == 0 else v

    def transform(which, ft):
        a = jnp.concatenate([lhs[which], lhs[which, :, :NT]], axis=1)
        return matmul(a, jnp.concatenate([fh[:, columns(ft)], fh[:, columns(ft)], fl[:, columns(ft)]], axis=0))

    def hats(ft):
        hat = transform(0, ft) * weight[:, columns(ft)]
        kh[0:SD, :, columns(ft)] = hat.reshape(SD, PD, 2 * LANES)
        km[0:SD, :, ft * LANES : (ft + 1) * LANES] = (hat[:, :LANES] - hat[:, LANES:]).reshape(SD, PD, LANES)
        vh[:, :, columns(ft)] = transform(1, ft).reshape(K, PD, 2 * LANES)

    def product(ft):
        re, im = parts(ft)
        for s0 in range(0, SD, 2):
            acc = [[None] * K for _ in range(6)]
            for p in range(PD // 8):
                rows = pl.ds(p * 8, 8)
                right = []
                for j in range(2):
                    c, d = kh[s0 + j, rows, re], kh[s0 + j, rows, im]
                    right.append((c, d, c + d))
                for k in range(K):
                    a, b = vh[VECTORS[k], rows, re], vh[VECTORS[k], rows, im]
                    left = (a, b, a + b)
                    for j in range(2):
                        for q in range(3):
                            term = left[q] * right[j][q]
                            old = acc[j * 3 + q][k]
                            acc[j * 3 + q][k] = term if old is None else old + term
            for j in range(2):
                p1, p2, p3 = (
                    jnp.concatenate([jnp.sum(v, axis=0, keepdims=True) for v in acc[j * 3 + q]], axis=0)
                    for q in range(3)
                )
                rows = pl.ds((s0 + j) * 8, 8)
                ph[rows, re] = keep(ft, p1 - p2, p1)
                ph[rows, im] = keep(ft, p3 - p1 - p2, p2)

    with phase("p_load"):
        loads[0].wait()
        high, low = split(kern[...].reshape(SD * PD, NT))
        lhs[0, :, :NT] = high
        lhs[0, :, NT:] = low
        loads[3].wait()
        high, low = split(vec[...].reshape(K * PD, NT))
        lhs[1, :, :NT] = high
        lhs[1, :, NT:] = low
        loads[1].wait()
        loads[2].wait()
    with phase("p_front0"):
        hats(0)
    with phase("p_front1"):
        hats(1)
        product(0)
    with phase("p_front2"):
        hats(2)
        product(1)
    with phase("p_front3"):
        product(2)
    forward = jnp.concatenate([fh[...], fh[...], fl[...]], axis=0)
    inverse = jnp.concatenate([fh[...], fh[...], fl[...]], axis=1)
    with phase("p_inv"):
        pred = matmul_t(stack(ph[...]), inverse)
        for c in range(16):
            part[c] = pred[c * 4 : c * 4 + 4]

    with phase("p_bar"):
        pl.semaphore_wait(barrier, len(greet))

    rs = []
    for i, (dx, dy) in enumerate(PLANE):
        chunk, target = plane(dx, dy)
        rs.append(remote(part.at[chunk], rs_in.at[i], rs_send.at[i], rs_recv.at[i], {"pts": target}))
        rs[-1].start()
    halo = [
        remote(vec.at[sens, pl.ds(PD - COLS, COLS)], halo_lo, halo_send.at[0], halo_recv.at[0], {"pts": up}),
        remote(vec.at[sens, pl.ds(0, COLS)], halo_hi, halo_send.at[1], halo_recv.at[1], {"pts": down}),
    ]
    share = remote(kh.at[pl.ds(0, SD)], kh.at[pl.ds(SD, SD)], share_send, share_recv, {"sens": core_peer})
    for copy in halo + [share]:
        copy.start()

    for i in (4, 8, 9):
        loads[i].wait()
    sensor = own_chunk // 2
    scale = noise[sensor]
    mix_high, mix_low = split(corr[group[sensor]])
    mix = jnp.concatenate([mix_high, mix_high, mix_low], axis=1)

    total = part[own_chunk]
    with phase("p_rswait"):
        for i in range(len(PLANE) - 1, -1, -1):
            rs[i].wait_recv()
            total = total + rs_in[i]
    zsum[...] = total
    swap = remote(zsum, z_in, z_send, z_recv, {"pts": z_peer})
    swap.start()

    with phase("p_zwait"):
        swap.wait_recv()
    total = zsum[...] + z_in[...]
    tall = jnp.concatenate([total, jnp.zeros((12, NT), F32)], axis=0)
    mixed = matmul_t(stack(tall), mix)[:4]
    value = scale * (total + mixed)
    mine[...] = value
    slot = sensor + SD * ((half + core) % 2)
    home = resid.at[slot]
    ag = []
    for i, (dx, dy) in enumerate(PLANE):
        target = {"pts": plane(dx, dy)[1], "sens": zl * 2 + half}
        ag.append(remote(mine, home, ag_send.at[i], ag_recv.at[slot], target))
        ag[-1].start()
    beside = remote(mine, home, ag_send.at[len(PLANE)], ag_recv.at[slot], {"sens": core_peer})

    @pl.when(half == core)
    def _():
        resid[slot] = value

    @pl.when(half != core)
    def _():
        beside.start()

    with phase("p_prior"):
        for i in range(5, 8):
            loads[i].wait()
        for copy in halo:
            copy.wait_recv()
        q = lax.broadcasted_iota(jnp.int32, (PD + 2 * COLS, PD), 0)
        here = lax.broadcasted_iota(jnp.int32, (PD + 2 * COLS, PD), 1) + COLS
        local = nbr[...] - pts * PD + COLS
        links = coup[...]
        diagonal = stiff[...] + jnp.sum(links, axis=0, keepdims=True)
        pick = jnp.where(q == here, diagonal, 0.0)
        for j in range(4):
            pick = pick - jnp.where(q == local[j : j + 1], links[j : j + 1], 0.0)
        padded = jnp.concatenate([halo_lo[...], vec[sens], halo_hi[...]], axis=0)
        prior[...] = lax.dot_general(
            pick, padded, (((0,), (0,)), ((), ())),
            precision=lax.Precision.HIGHEST, preferred_element_type=F32,
        )

    with phase("p_share"):
        share.wait_recv()
        for s in range(SD, 2 * SD):
            for ft in range(FT):
                re, im = parts(ft)
                km[s, :, ft * LANES : (ft + 1) * LANES] = kh[s, :, re] - kh[s, :, im]

    with phase("p_agwait"):
        for i in range(2 * SD):

            @pl.when((half + core) % 2 * 2 * SD + (slot - i) * (slot - i) > 0)
            def _(i=i):
                remote(mine, resid.at[i], ag_send.at[0], ag_recv.at[i], {"sens": core_peer}).wait_recv()

    with phase("p_rdft"):
        rows = jnp.concatenate([resid[c] for c in range(2 * SD)], axis=0)
        hat = matmul(stack(rows), forward)
        for c in range(2 * FT):
            rh[c] = hat[:, c * LANES : (c + 1) * LANES]

    rows_sub = PD // SUB

    def line_copy(i, j):
        piece = pl.ds(j * rows_sub, rows_sub)
        seat = 3 * (1 - inner) if i == 0 else i
        return remote(
            line_out.at[i, piece], line_in.at[seat, piece], line_send.at[i, j], line_recv.at[seat, j],
            {"sens": heads[i] * 2 + core},
        )

    def line_arrival(i, j):
        piece = pl.ds(j * rows_sub, rows_sub)
        return remote(
            line_out.at[0, piece], line_in.at[i, piece], line_send.at[0, j], line_recv.at[i, j],
            {"sens": core_peer},
        )

    def adjoint(i):
        v, into = order[i], grads[i % 2]
        for ft in range(FT):
            re, im = parts(ft)
            acc = [None] * (PD // 8)
            for s in range(2 * SD):
                a = rh[2 * ft, pl.ds(s * 4 + v, 8, stride=0), :]
                b = rh[2 * ft + 1, pl.ds(s * 4 + v, 8, stride=0), :]
                ab = a + b
                for p in range(PD // 8):
                    rows = pl.ds(p * 8, 8)
                    terms = (a * kh[s, rows, re], b * kh[s, rows, im], ab * km[s, rows, ft * LANES : (ft + 1) * LANES])
                    acc[p] = terms if s == 0 else tuple(m + n for m, n in zip(acc[p], terms, strict=True))
            for p in range(PD // 8):
                p1, p2, p3 = acc[p]
                into[pl.ds(p * 8, 8), re] = keep(ft, p1 + p2, p1)
                into[pl.ds(p * 8, 8), im] = keep(ft, p3 - p1 + p2, p2)

    with phase("p_adj"):
        adjoint(0)
    for i in range(4):
        with phase("p_adj%d" % i):
            if i < 3:
                adjoint(i + 1)
            line_out[i] = matmul_t(stack(grads[i % 2][...]), inverse)
        if i < 2:
            for j in range(SUB):
                line_copy(i, j).start()
        if i == 2:

            @pl.when(inner == 0)
            def _():
                for j in range(SUB):
                    line_copy(2, j).start()

    with phase("p_relay"):

        @pl.when(inner == 1)
        def _():
            for j in range(SUB):
                line_arrival(3, j).wait_recv()
                piece = pl.ds(j * rows_sub, rows_sub)
                line_out[2, piece] = line_out[2, piece] + line_in[3, piece]
                line_copy(2, j).start()

    prior[...] = prior[...] + line_out[3]

    with phase("p_linewait"):

        @pl.when(inner == 1)
        def _():
            for j in range(SUB):
                line_arrival(0, j).wait_recv()
            prior[...] = prior[...] + line_in[0]

        for i in (1, 2):
            for j in range(SUB):
                line_arrival(i, j).wait_recv()
        out_ref[0] = prior[...] + line_in[1] + line_in[2]

    with phase("p_sends"):
        for copy in halo + rs + [swap, share] + ag + [line_copy(i, j) for i in range(3) for j in range(SUB)]:
            copy.wait_send()

        @pl.when(half != core)
        def _():
            beside.wait_send()


def local(kernel, vectors, noise_scale, sensor_group, correlation, stiffness, couplings, neighbors):
    high, low = table()
    anywhere = pl.BlockSpec(memory_space=pl.ANY)
    dma = pltpu.SemaphoreType.DMA
    count = len(PLANE)
    return pl.pallas_call(
        body,
        out_shape=jax.ShapeDtypeStruct((1, PD, NT), F32),
        in_specs=[anywhere] * 10,
        out_specs=pl.BlockSpec(memory_space=pltpu.VMEM),
        scratch_shapes=[
            pltpu.VMEM((SD, PD, NT), F32),
            pltpu.VMEM((K, PD, NT), F32),
            pltpu.VMEM((NB, NT, NT), F32),
            pltpu.VMEM((1, PD), F32),
            pltpu.VMEM((4, PD), F32),
            pltpu.VMEM((4, PD), jnp.int32),
            pltpu.VMEM((NT, F2), BF16),
            pltpu.VMEM((NT, F2), BF16),
            pltpu.SMEM((SD,), F32),
            pltpu.SMEM((SD,), jnp.int32),
            pltpu.VMEM((2, SD * PD, 2 * NT), BF16),
            pltpu.VMEM((2 * SD, PD, F2), F32),
            pltpu.VMEM((2 * SD, PD, NT), F32),
            pltpu.VMEM((K, PD, F2), F32),
            pltpu.VMEM((SD * K, F2), F32),
            pltpu.VMEM((16, 4, NT), F32),
            pltpu.VMEM((count, 4, NT), F32),
            pltpu.VMEM((4, NT), F32),
            pltpu.VMEM((4, NT), F32),
            pltpu.VMEM((4, NT), F32),
            pltpu.VMEM((16, 4, NT), F32),
            pltpu.VMEM((2 * FT, SD * K, LANES), F32),
            pltpu.VMEM((PD, F2), F32),
            pltpu.VMEM((PD, F2), F32),
            pltpu.VMEM((PD, NT), F32),
            pltpu.VMEM((COLS, NT), F32),
            pltpu.VMEM((COLS, NT), F32),
            pltpu.VMEM((4, PD, NT), F32),
            pltpu.VMEM((4, PD, NT), F32),
            dma((10,)),
            dma((2,)), dma((2,)),
            dma((count,)), dma((count,)),
            dma, dma,
            dma((count + 1,)), dma((2 * SD,)),
            dma, dma,
            dma((3, SUB)), dma((4, SUB)),
        ],
        compiler_params=pltpu.CompilerParams(collective_id=0, has_side_effects=True),
    )(
        kernel, vectors, noise_scale, sensor_group, correlation, stiffness.reshape(1, PD),
        couplings, neighbors, jnp.asarray(high), jnp.asarray(low),
    )


def solution(mesh):
    in_specs = (
        P("sens", "pts", None),
        P(None, "pts", None),
        P("sens"),
        P("sens"),
        P(),
        P("pts"),
        P(None, "pts"),
        P(None, "pts"),
    )
    return jax.shard_map(
        local, mesh=mesh, in_specs=in_specs, out_specs=P("sens", "pts", None), check_vma=False
    )
```

```python
import contextlib
import math

import jax
import jax.numpy as jnp
import numpy as np
from jax import lax
from jax.experimental import pallas as pl
from jax.experimental.pallas import tpu as pltpu
from jax.sharding import PartitionSpec as P

F32, BF16 = jnp.float32, jnp.bfloat16
phase = lambda name: contextlib.nullcontext()
K, NT, NB, SD, PD, COLS = 8, 384, 4, 8, 64, 16
F2 = 2 * NT
LANES = 128
FT = NT // LANES
VECTORS = (0, 2, 4, 6, 1, 3, 5, 7)
PIECES = ((0, 2), (2, 1))
RS_ORDER = ((2, 0), (2, 1), (1, 0), (3, 0), (1, 1), (3, 1), (0, 0), (0, 1))
PLANE = sorted(
    ((dx, dy) for dx in range(4) for dy in range(4) if dx or dy),
    key=lambda d: -(min(d[0], 4 - d[0]) + min(d[1], 4 - d[1])),
)


def table():
    t = np.arange(NT)
    angle = 2.0 * math.pi / F2 * (t[:, None] * t[None, :] % F2)
    second = -np.sin(angle)
    second[:, 0] = np.where(t % 2 == 0, 1.0, -1.0)
    parts = [np.cos(angle).reshape(NT, FT, 1, LANES), second.reshape(NT, FT, 1, LANES)]
    full = np.concatenate(parts, axis=2).reshape(NT, F2).astype(np.float32)
    high = full.astype(BF16)
    low = (full - high.astype(np.float32)).astype(BF16)
    return high, low


def split(x):
    high = x.astype(BF16)
    low = (x - high.astype(F32)).astype(BF16)
    return high, low


def stack(x):
    high, low = split(x)
    return jnp.concatenate([high, low, high], axis=1)


def matmul(a, b):
    return lax.dot_general(a, b, (((1,), (0,)), ((), ())), preferred_element_type=F32)


def matmul_t(a, b):
    return lax.dot_general(a, b, (((1,), (1,)), ((), ())), preferred_element_type=F32)


def body(
    kern_hbm, vec_hbm, noise_hbm, group_hbm, corr_hbm, stiff_hbm, coup_hbm, nbr_hbm, fh_hbm, fl_hbm,
    out_ref,
    kern, vec, corr, stiff, coup, nbr, fh, fl, noise, group, lhs, mix,
    kh, km, vh, ph, part, rs_in, zsum, z_in, mine, resid, rh, grad_a, grad_b, prior,
    halo_lo, halo_hi, line_out, line_in,
    load_sem, halo_send, halo_recv, rs_send, rs_recv, tell_send, tell_recv, z_send, z_recv, ag_send, ag_recv,
    share_send, share_recv, line_send, line_recv,
):
    pts, sens = lax.axis_index("pts"), lax.axis_index("sens")
    x, zh, y = pts % 4, pts // 4 % 2, pts // 8
    zl, core = sens // 2, sens % 2

    def plane(dx, dy):
        tx, ty = (x + dx) % 4, (y + dy) % 4
        return ty * 4 + tx, (ty * 2 + zh) * 4 + tx

    own_chunk = y * 4 + x
    z_peer = (y * 2 + 1 - zh) * 4 + x
    up, down = (pts + 1) % 32, (pts + 31) % 32
    core_peer = zl * 2 + 1 - core
    grads = (grad_a, grad_b)
    order = [3 - zl, (12 - 2 * zl) % 5, 3 - (12 - 2 * zl) % 5, zl]
    heads = [1 + zl % 2, order[1], order[2]]
    inner = zl * (3 - zl) // 2

    loads = [
        pltpu.make_async_copy(src, dst, load_sem.at[i])
        for i, (src, dst) in enumerate(
            [
                (kern_hbm, kern), (fh_hbm, fh), (fl_hbm, fl), (vec_hbm, vec), (corr_hbm, corr),
                (stiff_hbm, stiff), (coup_hbm, coup), (nbr_hbm, nbr), (noise_hbm, noise.at[0]), (group_hbm, group.at[0]),
            ]
        )
    ]
    for i in range(4):
        loads[i].start()

    barrier = pltpu.get_barrier_semaphore()
    greet = [{"pts": plane(dx, dy)[1]} for dx, dy in PLANE]
    greet += [{"pts": plane(dx, dy)[1], "sens": core_peer} for dx, dy in PLANE]
    greet += [{"pts": z_peer}, {"pts": up}, {"pts": down}, {"sens": core_peer}]
    greet += [{"sens": (zl + i) % 4 * 2 + core} for i in range(1, 4)]
    for target in greet:
        pl.semaphore_signal(barrier, inc=1, device_id=target, device_id_type=pl.DeviceIdType.MESH)

    def remote(src, dst, send, recv, target):
        return pltpu.make_async_remote_copy(
            src_ref=src, dst_ref=dst, send_sem=send, recv_sem=recv,
            device_id=target, device_id_type=pl.DeviceIdType.MESH,
        )

    freq = lax.broadcasted_iota(jnp.int32, (1, F2), 1)
    weight = jnp.where(freq * (freq - LANES) == 0, 1.0 / F2, 2.0 / F2).astype(F32)

    lane = lax.broadcasted_iota(jnp.int32, (8, LANES), 1)

    def columns(ft):
        return slice(ft * 2 * LANES, (ft + 1) * 2 * LANES)

    def parts(ft):
        return slice(ft * 2 * LANES, ft * 2 * LANES + LANES), slice(ft * 2 * LANES + LANES, (ft + 1) * 2 * LANES)

    def keep(ft, v, other):
        return jnp.where(lane > 0, v, other) if ft == 0 else v

    def hats(ft, i):
        which, first = i // 2, i % 2 * 4
        rows = slice(first * PD, (first + 4) * PD)
        a = jnp.concatenate([lhs[which, rows], lhs[which, rows, :NT]], axis=1)
        block = columns(ft)
        hat = matmul(a, jnp.concatenate([fh[:, block], fh[:, block], fl[:, block]], axis=0))
        if which == 0:
            hat = hat * weight[:, block]
            kh[first : first + 4, :, block] = hat.reshape(4, PD, 2 * LANES)
            km[first : first + 4, :, ft * LANES : (ft + 1) * LANES] = (hat[:, :LANES] - hat[:, LANES:]).reshape(4, PD, LANES)
        else:
            vh[first : first + 4, :, block] = hat.reshape(4, PD, 2 * LANES)

    def product(ft, i):
        re, im = parts(ft)
        s0 = 2 * i
        acc = [[None] * K for _ in range(6)]
        for p in range(PD // 8):
            rows = pl.ds(p * 8, 8)
            right = []
            for j in range(2):
                c, d = kh[s0 + j, rows, re], kh[s0 + j, rows, im]
                right.append((c, d, c + d))
            for k in range(K):
                a, b = vh[VECTORS[k], rows, re], vh[VECTORS[k], rows, im]
                left = (a, b, a + b)
                for j in range(2):
                    for q in range(3):
                        term = left[q] * right[j][q]
                        old = acc[j * 3 + q][k]
                        acc[j * 3 + q][k] = term if old is None else old + term
        for j in range(2):
            p1, p2, p3 = (
                jnp.concatenate([jnp.sum(v, axis=0, keepdims=True) for v in acc[j * 3 + q]], axis=0)
                for q in range(3)
            )
            rows = pl.ds((s0 + j) * 8, 8)
            ph[rows, re] = keep(ft, p1 - p2, p1)
            ph[rows, im] = keep(ft, p3 - p1 - p2, p2)

    def halve(which, rows):
        high, low = split(rows.reshape(SD * PD, NT))
        lhs[which, :, :NT] = high
        lhs[which, :, NT:] = low

    with phase("p_load"):
        loads[0].wait()
        halve(0, kern[...])
        loads[1].wait()
        loads[2].wait()
    for i in range(4, 10):
        loads[i].start()
    with phase("p_front0"):
        for i in range(2):
            hats(0, i)
        loads[3].wait()
        halve(1, vec[...])
        for i in range(2, 4):
            hats(0, i)
    with phase("p_front1"):
        for i in range(4):
            hats(1, i)
            product(0, i)
    with phase("p_front2"):
        for i in range(4):
            hats(2, i)
            product(1, i)
    with phase("p_front3"):
        for i in range(4):
            product(2, i)
    inverse = jnp.concatenate([fh[...], fh[...], fl[...]], axis=1)
    with phase("p_inv"):
        pred = matmul_t(stack(ph[...]), inverse)
        part[...] = pred.reshape(SD, K, NT)

    with phase("p_bar"):
        pl.semaphore_wait(barrier, len(greet))

    place = own_chunk
    theirs = place // SD
    rs, others = [], []
    distant = 1 - (y - 2 * core + 5) % 4 // 2
    for i, (dx, near) in enumerate(RS_ORDER):
        row, column = distant + near * (1 - 2 * distant), (x + dx) % 4
        s = row * 4 + column
        owner = core * SD + s
        target = {"pts": ((core * 2 + row) * 2 + zh) * 4 + column, "sens": zl * 2}
        rs.append(remote(part.at[s], rs_in.at[place], rs_send, rs_recv, target))
        others.append(core + (owner - place) * (owner - place) > 0)
        pl.when(others[i])(rs[i].start)

    halo = [
        remote(vec.at[sens, pl.ds(PD - COLS, COLS)], halo_lo, halo_send.at[0], halo_recv.at[0], {"pts": up}),
        remote(vec.at[sens, pl.ds(0, COLS)], halo_hi, halo_send.at[1], halo_recv.at[1], {"pts": down}),
    ]
    share = remote(kh.at[pl.ds(0, SD)], kh.at[pl.ds(SD, SD)], share_send, share_recv, {"sens": core_peer})
    for i in range(4, 10):
        loads[i].wait()
    tell = [
        remote(noise.at[0], noise.at[1], tell_send.at[0], tell_recv.at[0], {"sens": core_peer}),
        remote(group.at[0], group.at[1], tell_send.at[1], tell_recv.at[1], {"sens": core_peer}),
    ]
    for copy in tell + halo + [share]:
        copy.start()
    for copy in tell:
        copy.wait_recv()

    swap = remote(zsum, z_in, z_send, z_recv, {"pts": z_peer})
    ag = []
    for h in range(2):
        home = resid.at[place % SD + SD * ((theirs + h) % 2)]
        for i, (dx, dy) in enumerate(PLANE):
            target = {"pts": plane(dx, dy)[1], "sens": zl * 2 + h}
            ag.append(remote(mine.at[h], home, ag_send.at[h], ag_recv, target))
    ag.append(remote(mine.at[1], home, ag_send.at[1], ag_recv, {"sens": core_peer}))

    @pl.when(core == 0)
    def _():
        seat = lax.broadcasted_iota(jnp.int32, (1, SD), 1) == place % SD
        scale = jnp.sum(jnp.where(seat, jnp.where(theirs == 0, noise[0], noise[1]), 0.0), axis=1, keepdims=True)
        kind = jnp.sum(jnp.where(seat, jnp.where(theirs == 0, group[0], group[1]), 0), axis=1, keepdims=True)
        matrix = corr[0]
        for g in range(1, NB):
            matrix = jnp.where(kind == g, corr[g], matrix)
        mix_high, mix_low = split(matrix)
        mix[:, :NT] = mix_high
        mix[:, NT : 2 * NT] = mix_high
        mix[:, 2 * NT :] = mix_low

        @pl.when(theirs == 0)
        def _():
            rs_in[place] = part[place % SD]

        with phase("p_rswait"):
            for count in (15, 16):

                @pl.when(theirs == count - 15)
                def _(count=count):
                    rows = rs_in.at[pl.ds(0, count)]
                    remote(rows, rows, rs_send, rs_recv, {"pts": up}).wait_recv()

            total = rs_in[0]
            for i in range(1, 16):
                total = total + rs_in[i]
        zsum[...] = total
        swap.start()
        with phase("p_zwait"):
            swap.wait_recv()
        total = zsum[...] + z_in[...]
        tall = jnp.concatenate([total, jnp.zeros((8, NT), F32)], axis=0)
        value = scale * (total + matmul_t(stack(tall), mix[...])[:K])
        mine[0] = value[:4]
        mine[1] = value[4:]
        for copy in ag:
            copy.start()
        resid[place % SD + SD * theirs] = value[:4]

    with phase("p_prior"):
        for copy in halo:
            copy.wait_recv()
        q = lax.broadcasted_iota(jnp.int32, (PD + 2 * COLS, PD), 0)
        here = lax.broadcasted_iota(jnp.int32, (PD + 2 * COLS, PD), 1) + COLS
        local = nbr[...] - pts * PD + COLS
        links = coup[...]
        diagonal = stiff[...] + jnp.sum(links, axis=0, keepdims=True)
        pick = jnp.where(q == here, diagonal, 0.0)
        for j in range(4):
            pick = pick - jnp.where(q == local[j : j + 1], links[j : j + 1], 0.0)
        padded = jnp.concatenate([halo_lo[...], vec[sens], halo_hi[...]], axis=0)
        term = lax.dot_general(
            pick, padded, (((0,), (0,)), ((), ())),
            precision=lax.Precision.HIGHEST, preferred_element_type=F32,
        )
        for c in range(FT):
            prior[c] = term[:, c * LANES : (c + 1) * LANES]

    with phase("p_share"):
        share.wait_recv()
        for s in range(SD, 2 * SD):
            for ft in range(FT):
                re, im = parts(ft)
                km[s, :, ft * LANES : (ft + 1) * LANES] = kh[s, :, re] - kh[s, :, im]

    with phase("p_agwait"):
        for count in (15, 16):

            @pl.when(core == count - 15)
            def _(count=count):
                rows = resid.at[pl.ds(0, count)]
                remote(rows, rows, ag_send.at[0], ag_recv, {"sens": core_peer}).wait_recv()

    def line_copy(i, j):
        seat = 3 * (1 - inner) if i == 0 else i
        arrival = (1 - inner) * (3 + j) if i == 0 else i
        return remote(
            line_out.at[i, j], line_in.at[seat, j], line_send.at[i], line_recv.at[arrival],
            {"sens": heads[i] * 2 + core},
        )

    def line_arrival(i):
        return remote(line_in.at[i], line_in.at[i], line_send.at[0], line_recv.at[i], {"sens": core_peer})

    def adjoint(i, fts=tuple(range(FT))):
        v, into = order[i], grads[i % 2]
        for ft in fts:
            re, im = parts(ft)
            acc = [None] * (PD // 8)
            for s in range(2 * SD):
                a = rh[2 * ft, pl.ds(s * 4 + v, 8, stride=0), :]
                b = rh[2 * ft + 1, pl.ds(s * 4 + v, 8, stride=0), :]
                ab = a + b
                for p in range(PD // 8):
                    rows = pl.ds(p * 8, 8)
                    terms = (a * kh[s, rows, re], b * kh[s, rows, im], ab * km[s, rows, ft * LANES : (ft + 1) * LANES])
                    acc[p] = terms if s == 0 else tuple(m + n for m, n in zip(acc[p], terms, strict=True))
            for p in range(PD // 8):
                p1, p2, p3 = acc[p]
                into[pl.ds(p * 8, 8), re] = keep(ft, p1 + p2, p1)
                into[pl.ds(p * 8, 8), im] = keep(ft, p3 - p1 + p2, p2)

    with phase("p_adj0"):
        rows = stack(jnp.concatenate([resid[c] for c in range(2 * SD)], axis=0))
        for ft in range(FT):
            block = columns(ft)
            hat = matmul(rows, jnp.concatenate([fh[:, block], fh[:, block], fl[:, block]], axis=0))
            rh[2 * ft] = hat[:, :LANES]
            rh[2 * ft + 1] = hat[:, LANES:]
            adjoint(0, (ft,))
    for i in range(4):
        with phase("p_inv%d" % i):
            left = stack(grads[i % 2][...])
            for start, size in PIECES:
                data = matmul_t(left, inverse[start * LANES : (start + size) * LANES])
                for c in range(size):
                    line_out[i, start + c] = data[:, c * LANES : (c + 1) * LANES]
                    if i < 2:
                        line_copy(i, start + c).start()
            if i == 2:

                @pl.when(inner == 0)
                def _():
                    for j in range(FT):
                        line_copy(2, j).start()

        if i < 3:
            with phase("p_adj%d" % (i + 1)):

                @pl.when(core >= 0)
                def _(i=i):
                    adjoint(i + 1)

    with phase("p_relay"):

        @pl.when(inner == 1)
        def _():
            for j in range(FT):
                remote(line_in.at[3, j], line_in.at[3, j], line_send.at[0], line_recv.at[3 + j], {"sens": core_peer}).wait_recv()
                line_out[2, j] = line_out[2, j] + line_in[3, j]
                line_copy(2, j).start()

    prior[...] = prior[...] + line_out[3]

    with phase("p_linewait"):

        @pl.when(inner == 1)
        def _():
            with phase("p_lw0"):
                line_arrival(0).wait_recv()
            prior[...] = prior[...] + line_in[0]

        for i in (1, 2):
            with phase("p_lw%d" % i):
                line_arrival(i).wait_recv()
        for c in range(FT):
            out_ref[0, :, c * LANES : (c + 1) * LANES] = prior[c] + line_in[1, c] + line_in[2, c]

    with phase("p_sends"):
        for copy in halo + tell + [share]:
            copy.wait_send()
        for i in range(3):
            remote(line_out.at[i], line_out.at[i], line_send.at[i], line_recv.at[0], {"sens": core_peer}).wait_send()
        for count in (7, 8):

            @pl.when((core + theirs > 0) == (count == 8))
            def _(count=count):
                rows = part.at[pl.ds(0, count)]
                remote(rows, rows, rs_send, rs_recv, {"pts": up}).wait_send()

        @pl.when(core == 0)
        def _():
            swap.wait_send()
            for h in range(2):
                rows = resid.at[pl.ds(0, 15 + h)]
                remote(rows, rows, ag_send.at[h], ag_recv, {"sens": core_peer}).wait_send()


def local(kernel, vectors, noise_scale, sensor_group, correlation, stiffness, couplings, neighbors):
    high, low = table()
    anywhere = pl.BlockSpec(memory_space=pl.ANY)
    dma = pltpu.SemaphoreType.DMA
    return pl.pallas_call(
        body,
        out_shape=pltpu.VMEM((1, PD, NT), F32),
        in_specs=[anywhere] * 10,
        out_specs=pl.BlockSpec(memory_space=pltpu.VMEM),
        scratch_shapes=[
            pltpu.VMEM((SD, PD, NT), F32),
            pltpu.VMEM((K, PD, NT), F32),
            pltpu.VMEM((NB, NT, NT), F32),
            pltpu.VMEM((1, PD), F32),
            pltpu.VMEM((4, PD), F32),
            pltpu.VMEM((4, PD), jnp.int32),
            pltpu.VMEM((NT, F2), BF16),
            pltpu.VMEM((NT, F2), BF16),
            pltpu.VMEM((2, 1, SD), F32),
            pltpu.VMEM((2, 1, SD), jnp.int32),
            pltpu.VMEM((2, SD * PD, 2 * NT), BF16),
            pltpu.VMEM((NT, 3 * NT), BF16),
            pltpu.VMEM((2 * SD, PD, F2), F32),
            pltpu.VMEM((2 * SD, PD, NT), F32),
            pltpu.VMEM((K, PD, F2), F32),
            pltpu.VMEM((SD * K, F2), F32),
            pltpu.VMEM((SD, K, NT), F32),
            pltpu.VMEM((16, K, NT), F32),
            pltpu.VMEM((K, NT), F32),
            pltpu.VMEM((K, NT), F32),
            pltpu.VMEM((2, 4, NT), F32),
            pltpu.VMEM((16, 4, NT), F32),
            pltpu.VMEM((2 * FT, SD * K, LANES), F32),
            pltpu.VMEM((PD, F2), F32),
            pltpu.VMEM((PD, F2), F32),
            pltpu.VMEM((FT, PD, LANES), F32),
            pltpu.VMEM((COLS, NT), F32),
            pltpu.VMEM((COLS, NT), F32),
            pltpu.VMEM((4, FT, PD, LANES), F32),
            pltpu.VMEM((4, FT, PD, LANES), F32),
            dma((10,)),
            dma((2,)), dma((2,)),
            dma, dma,
            dma((2,)), dma((2,)),
            dma, dma,
            dma((2,)), dma,
            dma, dma,
            dma((3,)), dma((3 + FT,)),
        ],
        compiler_params=pltpu.CompilerParams(collective_id=0, has_side_effects=True),
    )(
        kernel, vectors, noise_scale.reshape(1, SD), sensor_group.reshape(1, SD), correlation, stiffness.reshape(1, PD),
        couplings, neighbors, jnp.asarray(high), jnp.asarray(low),
    )


def solution(mesh):
    in_specs = (
        P("sens", "pts", None),
        P(None, "pts", None),
        P("sens"),
        P("sens"),
        P(),
        P("pts"),
        P(None, "pts"),
        P(None, "pts"),
    )
    return jax.shard_map(
        local, mesh=mesh, in_specs=in_specs, out_specs=P("sens", "pts", None), check_vma=False
    )
```

```python
import contextlib
import math

import jax
import jax.numpy as jnp
import numpy as np
from jax import lax
from jax.experimental import pallas as pl
from jax.experimental.pallas import tpu as pltpu
from jax.sharding import PartitionSpec as P

F32, BF16 = jnp.float32, jnp.bfloat16
phase = lambda name: contextlib.nullcontext()
K, NT, NB, SD, PD, COLS = 8, 384, 4, 8, 64, 16
F2 = 2 * NT
LANES = 128
FT = NT // LANES
VECTORS = (0, 2, 4, 6, 1, 3, 5, 7)
RS_ORDER = ((2, 0), (2, 1), (1, 0), (3, 0), (1, 1), (3, 1), (0, 0), (0, 1))
PLANE = sorted(
    ((dx, dy) for dx in range(4) for dy in range(4) if dx or dy),
    key=lambda d: -(min(d[0], 4 - d[0]) + min(d[1], 4 - d[1])),
)


def table():
    t = np.arange(NT)
    angle = 2.0 * math.pi / F2 * (t[:, None] * t[None, :] % F2)
    second = -np.sin(angle)
    second[:, 0] = np.where(t % 2 == 0, 1.0, -1.0)
    blocks = np.stack([np.cos(angle).reshape(NT, FT, LANES), second.reshape(NT, FT, LANES)], axis=2)
    full = blocks.reshape(NT, FT, 2 * LANES).transpose(1, 0, 2).astype(np.float32)
    high = full.astype(BF16)
    low = (full - high.astype(np.float32)).astype(BF16)
    both = np.stack([high, low], axis=1)
    return both, np.ascontiguousarray(both.transpose(0, 1, 3, 2))


def split(x):
    high = x.astype(BF16)
    low = (x - high.astype(F32)).astype(BF16)
    return high, low


def stack(x):
    high, low = split(x)
    return jnp.concatenate([high, low, high], axis=1)


def matmul(a, b):
    return lax.dot_general(a, b, (((1,), (0,)), ((), ())), preferred_element_type=F32)


def matmul_t(a, b):
    return lax.dot_general(a, b, (((1,), (1,)), ((), ())), preferred_element_type=F32)


def body(
    kern_hbm, vec_hbm, noise_hbm, group_hbm, corr_hbm, stiff_hbm, coup_hbm, nbr_hbm, fwd_hbm, inv_hbm,
    out_ref,
    kern, vec, corr, stiff, coup, nbr, fwd, inv, noise, group, lhs, mix,
    kh, km, vh, ph, part, rs_in, zsum, z_in, mine, resid, rh, grad_a, grad_b, prior,
    halo_lo, halo_hi, line_out, line_in, aid, aid_out,
    load_sem, halo_send, halo_recv, rs_send, rs_recv, tell_send, tell_recv, z_send, z_recv, ag_send, ag_recv,
    share_send, share_recv, line_send, line_recv, aid_recv,
):
    pts, sens = lax.axis_index("pts"), lax.axis_index("sens")
    x, zh, y = pts % 4, pts // 4 % 2, pts // 8
    zl, core = sens // 2, sens % 2

    def plane(dx, dy):
        tx, ty = (x + dx) % 4, (y + dy) % 4
        return ty * 4 + tx, (ty * 2 + zh) * 4 + tx

    own_chunk = y * 4 + x
    z_peer = (y * 2 + 1 - zh) * 4 + x
    up, down = (pts + 1) % 32, (pts + 31) % 32
    core_peer = zl * 2 + 1 - core
    grads = (grad_a, grad_b)
    order = [3 - zl, (12 - 2 * zl) % 5, 3 - (12 - 2 * zl) % 5, zl]
    heads = [1 + zl % 2, order[1], order[2]]
    inner = zl * (3 - zl) // 2

    loads = [
        pltpu.make_async_copy(src, dst, load_sem.at[i])
        for i, (src, dst) in enumerate(
            [
                (kern_hbm.at[pl.ds(0, 4)], kern.at[pl.ds(0, 4)]), (fwd_hbm.at[0], fwd.at[0]),
                (kern_hbm.at[pl.ds(4, 4)], kern.at[pl.ds(4, 4)]), (fwd_hbm.at[pl.ds(1, 2)], fwd.at[pl.ds(1, 2)]),
                (vec_hbm, vec), (inv_hbm, inv), (corr_hbm, corr),
                (stiff_hbm, stiff), (coup_hbm, coup), (nbr_hbm, nbr), (noise_hbm, noise.at[0]), (group_hbm, group.at[0]),
            ]
        )
    ]
    for i in range(5):
        loads[i].start()

    barrier = pltpu.get_barrier_semaphore()
    greet = [{"pts": plane(dx, dy)[1]} for dx, dy in PLANE]
    greet += [{"pts": plane(dx, dy)[1], "sens": core_peer} for dx, dy in PLANE]
    greet += [{"pts": z_peer}, {"pts": up}, {"pts": down}, {"sens": core_peer}]
    greet += [{"sens": (zl + i) % 4 * 2 + c} for i in range(1, 4) for c in (core, 1 - core)]
    for target in greet:
        pl.semaphore_signal(barrier, inc=1, device_id=target, device_id_type=pl.DeviceIdType.MESH)

    def remote(src, dst, send, recv, target):
        return pltpu.make_async_remote_copy(
            src_ref=src, dst_ref=dst, send_sem=send, recv_sem=recv,
            device_id=target, device_id_type=pl.DeviceIdType.MESH,
        )

    freq = lax.broadcasted_iota(jnp.int32, (1, F2), 1)
    weight = jnp.where(freq * (freq - LANES) == 0, 1.0 / F2, 2.0 / F2).astype(F32)

    lane = lax.broadcasted_iota(jnp.int32, (8, LANES), 1)

    def columns(ft):
        return slice(ft * 2 * LANES, (ft + 1) * 2 * LANES)

    def parts(ft):
        return slice(ft * 2 * LANES, ft * 2 * LANES + LANES), slice(ft * 2 * LANES + LANES, (ft + 1) * 2 * LANES)

    def forward(ft):
        return jnp.concatenate([fwd[ft, 0], fwd[ft, 0], fwd[ft, 1]], axis=0)

    def inverse(v, ft):
        return matmul(stack(v), jnp.concatenate([inv[ft, 0], inv[ft, 0], inv[ft, 1]], axis=0))

    def keep(ft, v, other):
        return jnp.where(lane > 0, v, other) if ft == 0 else v

    def hats(ft, i):
        which, first = i // 2, i % 2 * 4
        rows = slice(first * PD, (first + 4) * PD)
        a = jnp.concatenate([lhs[which, rows], lhs[which, rows, :NT]], axis=1)
        block = columns(ft)
        hat = matmul(a, forward(ft))
        if which == 0:
            hat = hat * weight[:, block]
            kh[first : first + 4, :, block] = hat.reshape(4, PD, 2 * LANES)
            km[first : first + 4, :, ft * LANES : (ft + 1) * LANES] = (hat[:, :LANES] - hat[:, LANES:]).reshape(4, PD, LANES)
        else:
            vh[first : first + 4, :, block] = hat.reshape(4, PD, 2 * LANES)

    def product(ft, i):
        re, im = parts(ft)
        s0 = 2 * i
        acc = [[None] * K for _ in range(6)]
        for p in range(PD // 8):
            rows = pl.ds(p * 8, 8)
            right = []
            for j in range(2):
                c, d = kh[s0 + j, rows, re], kh[s0 + j, rows, im]
                right.append((c, d, c + d))
            for k in range(K):
                a, b = vh[VECTORS[k], rows, re], vh[VECTORS[k], rows, im]
                left = (a, b, a + b)
                for j in range(2):
                    for q in range(3):
                        term = left[q] * right[j][q]
                        old = acc[j * 3 + q][k]
                        acc[j * 3 + q][k] = term if old is None else old + term
        for j in range(2):
            p1, p2, p3 = (
                jnp.concatenate([jnp.sum(v, axis=0, keepdims=True) for v in acc[j * 3 + q]], axis=0)
                for q in range(3)
            )
            rows = pl.ds((s0 + j) * 8, 8)
            ph[rows, re] = keep(ft, p1 - p2, p1)
            ph[rows, im] = keep(ft, p3 - p1 - p2, p2)

    def halve(which, first, rows):
        high, low = split(rows.reshape(-1, NT))
        lhs[which, first : first + high.shape[0], :NT] = high
        lhs[which, first : first + high.shape[0], NT:] = low

    with phase("p_load"):
        loads[0].wait()
        halve(0, 0, kern[0:4])
        loads[1].wait()
    with phase("p_front0"):
        hats(0, 0)
        loads[2].wait()
        halve(0, 4 * PD, kern[4:8])
        hats(0, 1)
        loads[3].wait()
        loads[4].wait()
        for i in range(5, 12):
            loads[i].start()
        halve(1, 0, vec[...])
        hats(1, 0)
        hats(1, 1)
        hats(0, 2)
        hats(0, 3)
    with phase("p_front1"):
        for i, (ft, rows) in enumerate(((1, 2), (1, 3), (2, 0), (2, 1))):
            hats(ft, rows)
            product(0, i)
    loads[5].wait()
    with phase("p_front2"):
        hats(2, 2)
        product(1, 0)
        product(1, 1)
        hats(2, 3)
        product(1, 2)
        pred = inverse(ph[:, columns(0)], 0)
        product(1, 3)
    with phase("p_front3"):
        product(2, 0)
        product(2, 1)
        pred = pred + inverse(ph[:, columns(1)], 1)
        product(2, 2)
        product(2, 3)
    with phase("p_inv"):
        pred = pred + inverse(ph[:, columns(2)], 2)
        part[...] = pred.reshape(SD, K, NT)

    with phase("p_bar"):
        pl.semaphore_wait(barrier, len(greet))

    place = own_chunk
    theirs = place // SD
    rs, others = [], []
    distant = 1 - (y - 2 * core + 5) % 4 // 2
    for i, (dx, near) in enumerate(RS_ORDER):
        row, column = distant + near * (1 - 2 * distant), (x + dx) % 4
        s = row * 4 + column
        owner = core * SD + s
        target = {"pts": ((core * 2 + row) * 2 + zh) * 4 + column, "sens": zl * 2}
        rs.append(remote(part.at[s], rs_in.at[place], rs_send, rs_recv, target))
        others.append(core + (owner - place) * (owner - place) > 0)
        pl.when(others[i])(rs[i].start)

    halo = [
        remote(vec.at[sens, pl.ds(PD - COLS, COLS)], halo_lo, halo_send.at[0], halo_recv.at[0], {"pts": up}),
        remote(vec.at[sens, pl.ds(0, COLS)], halo_hi, halo_send.at[1], halo_recv.at[1], {"pts": down}),
    ]
    share = remote(kh.at[pl.ds(0, SD)], kh.at[pl.ds(SD, SD)], share_send, share_recv, {"sens": core_peer})
    for i in range(6, 12):
        loads[i].wait()
    tell = [
        remote(noise.at[0], noise.at[1], tell_send.at[0], tell_recv.at[0], {"sens": core_peer}),
        remote(group.at[0], group.at[1], tell_send.at[1], tell_recv.at[1], {"sens": core_peer}),
    ]
    for copy in tell + halo + [share]:
        copy.start()
    for copy in tell:
        copy.wait_recv()

    swap = remote(zsum, z_in, z_send, z_recv, {"pts": z_peer})
    ag = []
    for h in range(2):
        home = resid.at[place % SD + SD * ((theirs + h) % 2)]
        for i, (dx, dy) in enumerate(PLANE):
            target = {"pts": plane(dx, dy)[1], "sens": zl * 2 + h}
            ag.append(remote(mine.at[h], home, ag_send.at[h], ag_recv, target))
    ag.append(remote(mine.at[1], home, ag_send.at[1], ag_recv, {"sens": core_peer}))

    @pl.when(core == 0)
    def _():
        seat = lax.broadcasted_iota(jnp.int32, (1, SD), 1) == place % SD
        scale = jnp.sum(jnp.where(seat, jnp.where(theirs == 0, noise[0], noise[1]), 0.0), axis=1, keepdims=True)
        kind = jnp.sum(jnp.where(seat, jnp.where(theirs == 0, group[0], group[1]), 0), axis=1, keepdims=True)
        matrix = corr[0]
        for g in range(1, NB):
            matrix = jnp.where(kind == g, corr[g], matrix)
        mix_high, mix_low = split(matrix)
        mix[:, :NT] = mix_high
        mix[:, NT : 2 * NT] = mix_high
        mix[:, 2 * NT :] = mix_low

        @pl.when(theirs == 0)
        def _():
            rs_in[place] = part[place % SD]

        with phase("p_rswait"):
            for count in (15, 16):

                @pl.when(theirs == count - 15)
                def _(count=count):
                    rows = rs_in.at[pl.ds(0, count)]
                    remote(rows, rows, rs_send, rs_recv, {"pts": up}).wait_recv()

            total = rs_in[0]
            for i in range(1, 16):
                total = total + rs_in[i]
        zsum[...] = total
        swap.start()
        with phase("p_zwait"):
            swap.wait_recv()
        total = zsum[...] + z_in[...]
        tall = jnp.concatenate([total, jnp.zeros((8, NT), F32)], axis=0)
        value = scale * (total + matmul_t(stack(tall), mix[...])[:K])
        mine[0] = value[:4]
        mine[1] = value[4:]
        for copy in ag:
            copy.start()
        resid[place % SD + SD * theirs] = value[:4]

    with phase("p_prior"):
        for copy in halo:
            copy.wait_recv()
        q = lax.broadcasted_iota(jnp.int32, (PD + 2 * COLS, PD), 0)
        here = lax.broadcasted_iota(jnp.int32, (PD + 2 * COLS, PD), 1) + COLS
        local = nbr[...] - pts * PD + COLS
        links = coup[...]
        diagonal = stiff[...] + jnp.sum(links, axis=0, keepdims=True)
        pick = jnp.where(q == here, diagonal, 0.0)
        for j in range(4):
            pick = pick - jnp.where(q == local[j : j + 1], links[j : j + 1], 0.0)
        padded = jnp.concatenate([halo_lo[...], vec[sens], halo_hi[...]], axis=0)
        term = lax.dot_general(
            pick, padded, (((0,), (0,)), ((), ())),
            precision=lax.Precision.HIGHEST, preferred_element_type=F32,
        )
        for c in range(FT):
            prior[c] = term[:, c * LANES : (c + 1) * LANES]

    with phase("p_share"):
        share.wait_recv()
        for s in range(SD, 2 * SD):
            for ft in range(FT):
                re, im = parts(ft)
                km[s, :, ft * LANES : (ft + 1) * LANES] = kh[s, :, re] - kh[s, :, im]

    with phase("p_agwait"):
        for count in (15, 16):

            @pl.when(core == count - 15)
            def _(count=count):
                rows = resid.at[pl.ds(0, count)]
                remote(rows, rows, ag_send.at[0], ag_recv, {"sens": core_peer}).wait_recv()

    def line_copy(i, j):
        seat, arrival, to = i, i, core
        if i == 0:
            seat = (1 - inner) * (3 + core)
            arrival = (1 - inner) * (3 + core * FT + j)
            to = core * inner
        return remote(
            line_out.at[i, j], line_in.at[seat, j], line_send.at[i], line_recv.at[arrival], {"sens": heads[i] * 2 + to}
        )

    assist = remote(line_out.at[2], aid, line_send.at[2], aid_recv, {"sens": core_peer})

    def line_arrival(i):
        return remote(line_in.at[i], line_in.at[i], line_send.at[0], line_recv.at[i], {"sens": core_peer})

    def adjoint(i, ft):
        v, into = order[i], grads[i % 2]
        re, im = parts(ft)
        acc = [None] * (PD // 8)
        for s in range(2 * SD):
            a = rh[2 * ft, pl.ds(s * 4 + v, 8, stride=0), :]
            b = rh[2 * ft + 1, pl.ds(s * 4 + v, 8, stride=0), :]
            ab = a + b
            for p in range(PD // 8):
                rows = pl.ds(p * 8, 8)
                terms = (a * kh[s, rows, re], b * kh[s, rows, im], ab * km[s, rows, ft * LANES : (ft + 1) * LANES])
                acc[p] = terms if s == 0 else tuple(m + n for m, n in zip(acc[p], terms, strict=True))
        for p in range(PD // 8):
            p1, p2, p3 = acc[p]
            into[pl.ds(p * 8, 8), re] = keep(ft, p1 + p2, p1)
            into[pl.ds(p * 8, 8), im] = keep(ft, p3 - p1 + p2, p2)

    def invert(i, ft):
        return inverse(grads[i % 2][:, columns(ft)], ft)

    for i in range(4):
        with phase("p_adj%d" % i):
            if i == 0:
                rows = stack(jnp.concatenate([resid[c] for c in range(2 * SD)], axis=0))

                def spectrum(ft):
                    hat = matmul(rows, forward(ft))
                    rh[2 * ft] = hat[:, :LANES]
                    rh[2 * ft + 1] = hat[:, LANES:]

                spectrum(0)
                spectrum(1)
            adjoint(i, 0)
            if i == 0:
                spectrum(2)
            adjoint(i, 1)
            data = invert(i, 0)
            adjoint(i, 2)
            data = data + invert(i, 1)
            data = data + invert(i, 2)
            for c in range(FT):
                line_out[i, c] = data[:, c * LANES : (c + 1) * LANES]
                if i < 2:
                    line_copy(i, c).start()
        if i == 2:

            @pl.when(core * inner == 1)
            def _():
                assist.start()

            @pl.when(inner == 0)
            def _():
                for j in range(FT):
                    line_copy(2, j).start()

    with phase("p_relay"):

        @pl.when((1 - core) * inner == 1)
        def _():
            assist.wait_recv()
            for j in range(FT):
                for c, mine_out in ((0, line_out.at[2, j]), (1, aid_out.at[j])):
                    came = line_in.at[3 + c, j]
                    remote(came, came, line_send.at[0], line_recv.at[3 + c * FT + j], {"sens": core_peer}).wait_recv()
                    mine_out[...] = came[...] + (aid[j] if c else line_out[2, j])
                    remote(
                        mine_out, line_in.at[2, j], line_send.at[2 + c], line_recv.at[2], {"sens": heads[2] * 2 + c}
                    ).start()

    prior[...] = prior[...] + line_out[3]

    with phase("p_linewait"):

        @pl.when(inner == 1)
        def _():
            with phase("p_lw0"):
                line_arrival(0).wait_recv()
            prior[...] = prior[...] + line_in[0]

        for i in (1, 2):
            with phase("p_lw%d" % i):
                line_arrival(i).wait_recv()
        for c in range(FT):
            out_ref[0, :, c * LANES : (c + 1) * LANES] = prior[c] + line_in[1, c] + line_in[2, c]

    with phase("p_sends"):
        for copy in halo + tell + [share]:
            copy.wait_send()
        for i in range(3):
            remote(line_out.at[i], line_out.at[i], line_send.at[i], line_recv.at[0], {"sens": core_peer}).wait_send()
        for count in (7, 8):

            @pl.when((core + theirs > 0) == (count == 8))
            def _(count=count):
                rows = part.at[pl.ds(0, count)]
                remote(rows, rows, rs_send, rs_recv, {"pts": up}).wait_send()

        @pl.when(core == 0)
        def _():
            swap.wait_send()

            @pl.when(inner == 1)
            def _():
                remote(aid_out, aid_out, line_send.at[3], line_recv.at[0], {"sens": core_peer}).wait_send()

            for h in range(2):
                rows = resid.at[pl.ds(0, 15 + h)]
                remote(rows, rows, ag_send.at[h], ag_recv, {"sens": core_peer}).wait_send()


def local(kernel, vectors, noise_scale, sensor_group, correlation, stiffness, couplings, neighbors):
    ahead, back = table()
    anywhere = pl.BlockSpec(memory_space=pl.ANY)
    dma = pltpu.SemaphoreType.DMA
    return pl.pallas_call(
        body,
        out_shape=pltpu.VMEM((1, PD, NT), F32),
        in_specs=[anywhere] * 10,
        out_specs=pl.BlockSpec(memory_space=pltpu.VMEM),
        scratch_shapes=[
            pltpu.VMEM((SD, PD, NT), F32),
            pltpu.VMEM((K, PD, NT), F32),
            pltpu.VMEM((NB, NT, NT), F32),
            pltpu.VMEM((1, PD), F32),
            pltpu.VMEM((4, PD), F32),
            pltpu.VMEM((4, PD), jnp.int32),
            pltpu.VMEM((FT, 2, NT, 2 * LANES), BF16),
            pltpu.VMEM((FT, 2, 2 * LANES, NT), BF16),
            pltpu.VMEM((2, 1, SD), F32),
            pltpu.VMEM((2, 1, SD), jnp.int32),
            pltpu.VMEM((2, SD * PD, 2 * NT), BF16),
            pltpu.VMEM((NT, 3 * NT), BF16),
            pltpu.VMEM((2 * SD, PD, F2), F32),
            pltpu.VMEM((2 * SD, PD, NT), F32),
            pltpu.VMEM((K, PD, F2), F32),
            pltpu.VMEM((SD * K, F2), F32),
            pltpu.VMEM((SD, K, NT), F32),
            pltpu.VMEM((16, K, NT), F32),
            pltpu.VMEM((K, NT), F32),
            pltpu.VMEM((K, NT), F32),
            pltpu.VMEM((2, 4, NT), F32),
            pltpu.VMEM((16, 4, NT), F32),
            pltpu.VMEM((2 * FT, SD * K, LANES), F32),
            pltpu.VMEM((PD, F2), F32),
            pltpu.VMEM((PD, F2), F32),
            pltpu.VMEM((FT, PD, LANES), F32),
            pltpu.VMEM((COLS, NT), F32),
            pltpu.VMEM((COLS, NT), F32),
            pltpu.VMEM((4, FT, PD, LANES), F32),
            pltpu.VMEM((5, FT, PD, LANES), F32),
            pltpu.VMEM((FT, PD, LANES), F32),
            pltpu.VMEM((FT, PD, LANES), F32),
            dma((12,)),
            dma((2,)), dma((2,)),
            dma, dma,
            dma((2,)), dma((2,)),
            dma, dma,
            dma((2,)), dma,
            dma, dma,
            dma((4,)), dma((3 + 2 * FT,)), dma,
        ],
        compiler_params=pltpu.CompilerParams(collective_id=0, has_side_effects=True),
    )(
        kernel, vectors, noise_scale.reshape(1, SD), sensor_group.reshape(1, SD), correlation, stiffness.reshape(1, PD),
        couplings, neighbors, jnp.asarray(ahead), jnp.asarray(back),
    )


def solution(mesh):
    in_specs = (
        P("sens", "pts", None),
        P(None, "pts", None),
        P("sens"),
        P("sens"),
        P(),
        P("pts"),
        P(None, "pts"),
        P(None, "pts"),
    )
    return jax.shard_map(
        local, mesh=mesh, in_specs=in_specs, out_specs=P("sens", "pts", None), check_vma=False
    )
```

```python
import contextlib
import math

import jax
import jax.numpy as jnp
import numpy as np
from jax import lax
from jax.experimental import pallas as pl
from jax.experimental.pallas import tpu as pltpu
from jax.sharding import PartitionSpec as P

F32, BF16 = jnp.float32, jnp.bfloat16
phase = lambda name: contextlib.nullcontext()
K, NT, NB, SD, PD, COLS = 8, 384, 4, 8, 64, 16
F2 = 2 * NT
LANES = 128
FT = NT // LANES
VECTORS = (0, 2, 4, 6, 1, 3, 5, 7)
TURNS = (((1, 0),), ((0, 0),), ((1, 1),), ((0, 1),))
RS_ORDER = ((2, 0), (2, 1), (1, 0), (3, 0), (1, 1), (3, 1), (0, 0), (0, 1))
PLANE = sorted(
    ((dx, dy) for dx in range(4) for dy in range(4) if dx or dy),
    key=lambda d: -(min(d[0], 4 - d[0]) + min(d[1], 4 - d[1])),
)


def table():
    t = np.arange(NT)
    angle = 2.0 * math.pi / F2 * (t[:, None] * t[None, :] % F2)
    second = -np.sin(angle)
    second[:, 0] = np.where(t % 2 == 0, 1.0, -1.0)
    blocks = np.stack([np.cos(angle).reshape(NT, FT, LANES), second.reshape(NT, FT, LANES)], axis=2)
    full = blocks.reshape(NT, FT, 2 * LANES).transpose(1, 0, 2).astype(np.float32)
    high = full.astype(BF16)
    low = (full - high.astype(np.float32)).astype(BF16)
    both = np.stack([high, low], axis=1)
    return both, np.ascontiguousarray(both.transpose(0, 1, 3, 2))


def split(x):
    high = x.astype(BF16)
    low = (x - high.astype(F32)).astype(BF16)
    return high, low


def stack(x):
    high, low = split(x)
    return jnp.concatenate([high, low, high], axis=1)


def matmul(a, b):
    return lax.dot_general(a, b, (((1,), (0,)), ((), ())), preferred_element_type=F32)


def matmul_t(a, b):
    return lax.dot_general(a, b, (((1,), (1,)), ((), ())), preferred_element_type=F32)


def body(
    kern_hbm, vec_hbm, noise_hbm, group_hbm, corr_hbm, stiff_hbm, coup_hbm, nbr_hbm, fwd_hbm, inv_hbm,
    out_ref,
    kern, vec, corr, stiff, coup, nbr, fwd, inv, noise, group, lhs, mix,
    kh, km, vh, ph, part, rs_in, zsum, z_in, mine, resid, rh, grad_a, grad_b, prior,
    halo_lo, halo_hi, line_out, line_in, aid, aid_out,
    load_sem, halo_send, halo_recv, rs_send, rs_recv, tell_send, tell_recv, z_send, z_recv, ag_send, ag_recv,
    share_send, share_recv, line_send, line_recv, aid_recv,
):
    pts, sens = lax.axis_index("pts"), lax.axis_index("sens")
    x, zh, y = pts % 4, pts // 4 % 2, pts // 8
    zl, core = sens // 2, sens % 2

    def plane(dx, dy):
        tx, ty = (x + dx) % 4, (y + dy) % 4
        return ty * 4 + tx, (ty * 2 + zh) * 4 + tx

    own_chunk = y * 4 + x
    z_peer = (y * 2 + 1 - zh) * 4 + x
    up, down = (pts + 1) % 32, (pts + 31) % 32
    core_peer = zl * 2 + 1 - core
    grads = (grad_a, grad_b)
    is0, is3 = (3 - zl) // 3, zl // 3
    is1 = zl % 2 - is3
    is2 = 1 - is0 - is1 - is3
    inner = is1 + is2
    order = [3 * is0 + is2, 2 * is0 + 2 * is1 + 3 * is2 + 2 * is3, is0 + 3 * is1 + is3, zl]
    heads = [is0 + is2 + 2 * is3, order[1], order[2]]

    loads = [
        pltpu.make_async_copy(src, dst, load_sem.at[i])
        for i, (src, dst) in enumerate(
            [
                (kern_hbm, kern), (fwd_hbm.at[0], fwd.at[0]), (vec_hbm, vec),
                (fwd_hbm.at[pl.ds(1, 2)], fwd.at[pl.ds(1, 2)]), (inv_hbm, inv), (corr_hbm, corr),
                (stiff_hbm, stiff), (coup_hbm, coup), (nbr_hbm, nbr), (noise_hbm, noise.at[0]), (group_hbm, group.at[0]),
            ]
        )
    ]
    for i in range(4):
        loads[i].start()

    barrier = pltpu.get_barrier_semaphore()
    greet = [{"pts": plane(dx, dy)[1]} for dx, dy in PLANE]
    greet += [{"pts": plane(dx, dy)[1], "sens": core_peer} for dx, dy in PLANE]
    greet += [{"pts": z_peer}, {"pts": up}, {"pts": down}, {"sens": core_peer}]
    greet += [{"sens": (zl + i) % 4 * 2 + c} for i in range(1, 4) for c in (core, 1 - core)]
    for target in greet:
        pl.semaphore_signal(barrier, inc=1, device_id=target, device_id_type=pl.DeviceIdType.MESH)

    def remote(src, dst, send, recv, target):
        return pltpu.make_async_remote_copy(
            src_ref=src, dst_ref=dst, send_sem=send, recv_sem=recv,
            device_id=target, device_id_type=pl.DeviceIdType.MESH,
        )

    freq = lax.broadcasted_iota(jnp.int32, (1, F2), 1)
    weight = jnp.where(freq * (freq - LANES) == 0, 1.0 / F2, 2.0 / F2).astype(F32)

    lane = lax.broadcasted_iota(jnp.int32, (8, LANES), 1)

    def columns(ft):
        return slice(ft * 2 * LANES, (ft + 1) * 2 * LANES)

    def parts(ft):
        return slice(ft * 2 * LANES, ft * 2 * LANES + LANES), slice(ft * 2 * LANES + LANES, (ft + 1) * 2 * LANES)

    def forward(ft):
        return jnp.concatenate([fwd[ft, 0], fwd[ft, 0], fwd[ft, 1]], axis=0)

    def inverse(v, ft):
        return matmul(stack(v), jnp.concatenate([inv[ft, 0], inv[ft, 0], inv[ft, 1]], axis=0))

    def keep(ft, v, other):
        return jnp.where(lane > 0, v, other) if ft == 0 else v

    def hats(ft, i):
        which, first = i // 2, i % 2 * 4
        rows = slice(first * PD, (first + 4) * PD)
        a = jnp.concatenate([lhs[which, rows], lhs[which, rows, :NT]], axis=1)
        block = columns(ft)
        hat = matmul(a, forward(ft))
        if which == 0:
            hat = hat * weight[:, block]
            kh[first : first + 4, :, block] = hat.reshape(4, PD, 2 * LANES)
            km[first : first + 4, :, ft * LANES : (ft + 1) * LANES] = (hat[:, :LANES] - hat[:, LANES:]).reshape(4, PD, LANES)
        else:
            vh[first : first + 4, :, block] = hat.reshape(4, PD, 2 * LANES)

    def product(ft, i):
        re, im = parts(ft)
        s0 = 2 * i
        acc = [[None] * K for _ in range(6)]
        for p in range(PD // 8):
            rows = pl.ds(p * 8, 8)
            right = []
            for j in range(2):
                c, d = kh[s0 + j, rows, re], kh[s0 + j, rows, im]
                right.append((c, d, c + d))
            for k in range(K):
                a, b = vh[VECTORS[k], rows, re], vh[VECTORS[k], rows, im]
                left = (a, b, a + b)
                for j in range(2):
                    for q in range(3):
                        term = left[q] * right[j][q]
                        old = acc[j * 3 + q][k]
                        acc[j * 3 + q][k] = term if old is None else old + term
        for j in range(2):
            p1, p2, p3 = (
                jnp.concatenate([jnp.sum(v, axis=0, keepdims=True) for v in acc[j * 3 + q]], axis=0)
                for q in range(3)
            )
            rows = pl.ds((s0 + j) * 8, 8)
            ph[rows, re] = keep(ft, p1 - p2, p1)
            ph[rows, im] = keep(ft, p3 - p1 - p2, p2)

    def halve(which, first, rows):
        high, low = split(rows.reshape(-1, NT))
        lhs[which, first : first + high.shape[0], :NT] = high
        lhs[which, first : first + high.shape[0], NT:] = low

    with phase("p_load"):
        loads[0].wait()
        halve(0, 0, kern[...])
        loads[1].wait()
    with phase("p_front0"):
        for i in range(2):
            hats(0, i)
        loads[2].wait()
        loads[3].wait()
        for i in range(4, 11):
            loads[i].start()
        halve(1, 0, vec[...])
        for i in range(2, 4):
            hats(0, i)
    with phase("p_front1"):
        for i in range(4):
            hats(1, i)
            product(0, i)
    with phase("p_front2"):
        for i in range(4):
            hats(2, i)
            product(1, i)
        loads[4].wait()
    with phase("p_front3"):
        for i in range(4):
            product(2, i)
    with phase("p_inv"):
        pred = inverse(ph[:, columns(0)], 0) + inverse(ph[:, columns(1)], 1) + inverse(ph[:, columns(2)], 2)
        part[...] = pred.reshape(SD, K, NT)

    with phase("p_bar"):
        pl.semaphore_wait(barrier, len(greet))

    place = own_chunk
    theirs = place // SD
    rs, others = [], []
    distant = 1 - (y - 2 * core + 5) % 4 // 2
    for i, (dx, near) in enumerate(RS_ORDER):
        row, column = distant + near * (1 - 2 * distant), (x + dx) % 4
        s = row * 4 + column
        owner = core * SD + s
        target = {"pts": ((core * 2 + row) * 2 + zh) * 4 + column, "sens": zl * 2}
        rs.append(remote(part.at[s], rs_in.at[place], rs_send, rs_recv, target))
        others.append(core + (owner - place) * (owner - place) > 0)
        pl.when(others[i])(rs[i].start)

    halo = [
        remote(vec.at[sens, pl.ds(PD - COLS, COLS)], halo_lo, halo_send.at[0], halo_recv.at[0], {"pts": up}),
        remote(vec.at[sens, pl.ds(0, COLS)], halo_hi, halo_send.at[1], halo_recv.at[1], {"pts": down}),
    ]
    share = remote(kh.at[pl.ds(0, SD)], kh.at[pl.ds(SD, SD)], share_send, share_recv, {"sens": core_peer})
    for i in range(5, 11):
        loads[i].wait()
    tell = [
        remote(noise.at[0], noise.at[1], tell_send.at[0], tell_recv.at[0], {"sens": core_peer}),
        remote(group.at[0], group.at[1], tell_send.at[1], tell_recv.at[1], {"sens": core_peer}),
    ]
    for copy in tell + halo + [share]:
        copy.start()
    for copy in tell:
        copy.wait_recv()

    swap = remote(zsum, z_in, z_send, z_recv, {"pts": z_peer})
    ag = []
    for h in (0, 1):
        home = resid.at[place % SD + SD * ((theirs + h) % 2)]
        for i, (dx, dy) in enumerate(PLANE):
            target = {"pts": plane(dx, dy)[1], "sens": zl * 2 + h}
            ag.append(remote(mine.at[h], home, ag_send.at[h], ag_recv, target))
        if h:
            ag.append(remote(mine.at[1], home, ag_send.at[1], ag_recv, {"sens": core_peer}))

    @pl.when(core == 0)
    def _():
        seat = lax.broadcasted_iota(jnp.int32, (1, SD), 1) == place % SD
        scale = jnp.sum(jnp.where(seat, jnp.where(theirs == 0, noise[0], noise[1]), 0.0), axis=1, keepdims=True)
        kind = jnp.sum(jnp.where(seat, jnp.where(theirs == 0, group[0], group[1]), 0), axis=1, keepdims=True)
        matrix = corr[0]
        for g in range(1, NB):
            matrix = jnp.where(kind == g, corr[g], matrix)
        mix_high, mix_low = split(matrix)
        mix[:, :NT] = mix_high
        mix[:, NT : 2 * NT] = mix_high
        mix[:, 2 * NT :] = mix_low

        @pl.when(theirs == 0)
        def _():
            rs_in[place] = part[place % SD]

        with phase("p_rswait"):
            for count in (15, 16):

                @pl.when(theirs == count - 15)
                def _(count=count):
                    rows = rs_in.at[pl.ds(0, count)]
                    remote(rows, rows, rs_send, rs_recv, {"pts": up}).wait_recv()

            total = rs_in[0]
            for i in range(1, 16):
                total = total + rs_in[i]
        zsum[...] = total
        swap.start()
        with phase("p_zwait"):
            swap.wait_recv()
        total = zsum[...] + z_in[...]
        tall = jnp.concatenate([total, jnp.zeros((8, NT), F32)], axis=0)
        value = scale * (total + matmul_t(stack(tall), mix[...])[:K])
        mine[0] = value[:4]
        mine[1] = value[4:]
        for copy in ag:
            copy.start()
        resid[place % SD + SD * theirs] = value[:4]

    with phase("p_prior"):
        for copy in halo:
            copy.wait_recv()
        q = lax.broadcasted_iota(jnp.int32, (PD + 2 * COLS, PD), 0)
        here = lax.broadcasted_iota(jnp.int32, (PD + 2 * COLS, PD), 1) + COLS
        local = nbr[...] - pts * PD + COLS
        links = coup[...]
        diagonal = stiff[...] + jnp.sum(links, axis=0, keepdims=True)
        pick = jnp.where(q == here, diagonal, 0.0)
        for j in range(4):
            pick = pick - jnp.where(q == local[j : j + 1], links[j : j + 1], 0.0)
        padded = jnp.concatenate([halo_lo[...], vec[sens], halo_hi[...]], axis=0)
        term = lax.dot_general(
            pick, padded, (((0,), (0,)), ((), ())),
            precision=lax.Precision.HIGHEST, preferred_element_type=F32,
        )
        for c in range(FT):
            prior[c] = term[:, c * LANES : (c + 1) * LANES]

    with phase("p_share"):
        share.wait_recv()
        for s in range(SD, 2 * SD):
            for ft in range(FT):
                re, im = parts(ft)
                km[s, :, ft * LANES : (ft + 1) * LANES] = kh[s, :, re] - kh[s, :, im]

    with phase("p_agwait"):
        for count in (15, 16):

            @pl.when(core == count - 15)
            def _(count=count):
                rows = resid.at[pl.ds(0, count)]
                remote(rows, rows, ag_send.at[0], ag_recv, {"sens": core_peer}).wait_recv()

    def line_copy(i, j):
        seat, arrival, to = zl, zl, core
        if i == 0:
            seat = inner * zl + (1 - inner) * (4 + core)
            arrival = inner * zl + (1 - inner) * (4 + core * FT + j)
            to = core * inner
        return remote(
            line_out.at[i, j], line_in.at[seat, j], line_send.at[i], line_recv.at[arrival], {"sens": heads[i] * 2 + to}
        )

    assist = remote(line_out.at[2], aid, line_send.at[2], aid_recv, {"sens": core_peer})

    def line_arrival(i):
        return remote(line_in.at[i], line_in.at[i], line_send.at[0], line_recv.at[i], {"sens": core_peer})

    def adjoint(i, ft):
        v, into = order[i], grads[i % 2]
        re, im = parts(ft)
        acc = [None] * (PD // 8)
        for s in range(2 * SD):
            a = rh[2 * ft, pl.ds(s * 4 + v, 8, stride=0), :]
            b = rh[2 * ft + 1, pl.ds(s * 4 + v, 8, stride=0), :]
            ab = a + b
            for p in range(PD // 8):
                rows = pl.ds(p * 8, 8)
                terms = (a * kh[s, rows, re], b * kh[s, rows, im], ab * km[s, rows, ft * LANES : (ft + 1) * LANES])
                acc[p] = terms if s == 0 else tuple(m + n for m, n in zip(acc[p], terms, strict=True))
        for p in range(PD // 8):
            p1, p2, p3 = acc[p]
            into[pl.ds(p * 8, 8), re] = keep(ft, p1 + p2, p1)
            into[pl.ds(p * 8, 8), im] = keep(ft, p3 - p1 + p2, p2)

    def invert(i, ft):
        return inverse(grads[i % 2][:, columns(ft)], ft)

    for i in range(4):
        with phase("p_adj%d" % i):
            if i == 0:
                rows = stack(jnp.concatenate([resid[c] for c in range(2 * SD)], axis=0))

                def spectrum(ft):
                    hat = matmul(rows, forward(ft))
                    rh[2 * ft] = hat[:, :LANES]
                    rh[2 * ft + 1] = hat[:, LANES:]

                spectrum(0)
                spectrum(1)
            adjoint(i, 0)
            if i == 0:
                spectrum(2)
            adjoint(i, 1)
            data = invert(i, 0)
            adjoint(i, 2)
            data = data + invert(i, 1)
            data = data + invert(i, 2)
            for c in range(FT):
                line_out[i, c] = data[:, c * LANES : (c + 1) * LANES]

        for when, which in TURNS[i]:

            @pl.when(core == when)
            def _(which=which):
                for j in range(FT):
                    line_copy(which, j).start()

        if i == 2:

            @pl.when(core * inner == 1)
            def _():
                assist.start()

        if i == 3:

            @pl.when(inner == 0)
            def _():
                for j in range(FT):
                    line_copy(2, j).start()

    with phase("p_relay"):

        @pl.when((1 - core) * inner == 1)
        def _():
            assist.wait_recv()
            for c in (1, 0):
                for j in range(FT):
                    mine_out = aid_out.at[j] if c else line_out.at[2, j]
                    came = line_in.at[4 + c, j]
                    remote(came, came, line_send.at[0], line_recv.at[4 + c * FT + j], {"sens": core_peer}).wait_recv()
                    mine_out[...] = came[...] + (aid[j] if c else line_out[2, j])
                    remote(
                        mine_out, line_in.at[zl, j], line_send.at[2 + c], line_recv.at[zl], {"sens": heads[2] * 2 + c}
                    ).start()

    prior[...] = prior[...] + line_out[3]

    with phase("p_linewait"):

        @pl.when(inner == 1)
        def _():
            for i in (0, 3):
                line_arrival(i).wait_recv()
            prior[...] = prior[...] + line_in[0] + line_in[3]
            line_arrival(3 - zl).wait_recv()
            for c in range(FT):
                out_ref[0, :, c * LANES : (c + 1) * LANES] = prior[c] + line_in[3 - zl, c]

        @pl.when(inner == 0)
        def _():
            for i in (1, 2):
                line_arrival(i).wait_recv()
            for c in range(FT):
                out_ref[0, :, c * LANES : (c + 1) * LANES] = prior[c] + line_in[1, c] + line_in[2, c]

    with phase("p_sends"):
        for copy in halo + tell + [share]:
            copy.wait_send()
        for i in range(3):
            remote(line_out.at[i], line_out.at[i], line_send.at[i], line_recv.at[0], {"sens": core_peer}).wait_send()
        for count in (7, 8):

            @pl.when((core + theirs > 0) == (count == 8))
            def _(count=count):
                rows = part.at[pl.ds(0, count)]
                remote(rows, rows, rs_send, rs_recv, {"pts": up}).wait_send()

        @pl.when(core == 0)
        def _():
            swap.wait_send()

            @pl.when(inner == 1)
            def _():
                remote(aid_out, aid_out, line_send.at[3], line_recv.at[0], {"sens": core_peer}).wait_send()

            for h in range(2):
                rows = resid.at[pl.ds(0, 15 + h)]
                remote(rows, rows, ag_send.at[h], ag_recv, {"sens": core_peer}).wait_send()


def local(kernel, vectors, noise_scale, sensor_group, correlation, stiffness, couplings, neighbors):
    ahead, back = table()
    anywhere = pl.BlockSpec(memory_space=pl.ANY)
    dma = pltpu.SemaphoreType.DMA
    return pl.pallas_call(
        body,
        out_shape=pltpu.VMEM((1, PD, NT), F32),
        in_specs=[anywhere] * 10,
        out_specs=pl.BlockSpec(memory_space=pltpu.VMEM),
        scratch_shapes=[
            pltpu.VMEM((SD, PD, NT), F32),
            pltpu.VMEM((K, PD, NT), F32),
            pltpu.VMEM((NB, NT, NT), F32),
            pltpu.VMEM((1, PD), F32),
            pltpu.VMEM((4, PD), F32),
            pltpu.VMEM((4, PD), jnp.int32),
            pltpu.VMEM((FT, 2, NT, 2 * LANES), BF16),
            pltpu.VMEM((FT, 2, 2 * LANES, NT), BF16),
            pltpu.VMEM((2, 1, SD), F32),
            pltpu.VMEM((2, 1, SD), jnp.int32),
            pltpu.VMEM((2, SD * PD, 2 * NT), BF16),
            pltpu.VMEM((NT, 3 * NT), BF16),
            pltpu.VMEM((2 * SD, PD, F2), F32),
            pltpu.VMEM((2 * SD, PD, NT), F32),
            pltpu.VMEM((K, PD, F2), F32),
            pltpu.VMEM((SD * K, F2), F32),
            pltpu.VMEM((SD, K, NT), F32),
            pltpu.VMEM((16, K, NT), F32),
            pltpu.VMEM((K, NT), F32),
            pltpu.VMEM((K, NT), F32),
            pltpu.VMEM((2, 4, NT), F32),
            pltpu.VMEM((16, 4, NT), F32),
            pltpu.VMEM((2 * FT, SD * K, LANES), F32),
            pltpu.VMEM((PD, F2), F32),
            pltpu.VMEM((PD, F2), F32),
            pltpu.VMEM((FT, PD, LANES), F32),
            pltpu.VMEM((COLS, NT), F32),
            pltpu.VMEM((COLS, NT), F32),
            pltpu.VMEM((4, FT, PD, LANES), F32),
            pltpu.VMEM((6, FT, PD, LANES), F32),
            pltpu.VMEM((FT, PD, LANES), F32),
            pltpu.VMEM((FT, PD, LANES), F32),
            dma((11,)),
            dma((2,)), dma((2,)),
            dma, dma,
            dma((2,)), dma((2,)),
            dma, dma,
            dma((2,)), dma,
            dma, dma,
            dma((4,)), dma((4 + 2 * FT,)), dma,
        ],
        compiler_params=pltpu.CompilerParams(collective_id=0, has_side_effects=True),
    )(
        kernel, vectors, noise_scale.reshape(1, SD), sensor_group.reshape(1, SD), correlation, stiffness.reshape(1, PD),
        couplings, neighbors, jnp.asarray(ahead), jnp.asarray(back),
    )


def solution(mesh):
    in_specs = (
        P("sens", "pts", None),
        P(None, "pts", None),
        P("sens"),
        P("sens"),
        P(),
        P("pts"),
        P(None, "pts"),
        P(None, "pts"),
    )
    return jax.shard_map(
        local, mesh=mesh, in_specs=in_specs, out_specs=P("sens", "pts", None), check_vma=False
    )
```

```python
import contextlib
import math

import jax
import jax.numpy as jnp
import numpy as np
from jax import lax
from jax.experimental import pallas as pl
from jax.experimental.pallas import tpu as pltpu
from jax.sharding import PartitionSpec as P

F32, BF16 = jnp.float32, jnp.bfloat16
phase = lambda name: contextlib.nullcontext()
K, NT, NB, SD, PD, COLS = 8, 384, 4, 8, 64, 16
F2 = 2 * NT
LANES = 128
FT = NT // LANES
VECTORS = (0, 2, 4, 6, 1, 3, 5, 7)
TURNS = (((1, 0),), ((0, 0),), ((1, 1),), ((0, 1),))
RS_ORDER = ((2, 0), (2, 1), (1, 0), (3, 0), (1, 1), (3, 1), (0, 0), (0, 1))
PLANE = sorted(
    ((dx, dy) for dx in range(4) for dy in range(4) if dx or dy),
    key=lambda d: -(min(d[0], 4 - d[0]) + min(d[1], 4 - d[1])),
)


def table():
    t = np.arange(NT)
    angle = 2.0 * math.pi / F2 * (t[:, None] * t[None, :] % F2)
    second = -np.sin(angle)
    second[:, 0] = np.where(t % 2 == 0, 1.0, -1.0)
    blocks = np.stack([np.cos(angle).reshape(NT, FT, LANES), second.reshape(NT, FT, LANES)], axis=2)
    full = blocks.reshape(NT, FT, 2 * LANES).transpose(1, 0, 2).astype(np.float32)
    high = full.astype(BF16)
    low = (full - high.astype(np.float32)).astype(BF16)
    both = np.stack([high, low], axis=1)
    return both, np.ascontiguousarray(both.transpose(0, 1, 3, 2))


def split(x):
    high = x.astype(BF16)
    low = (x - high.astype(F32)).astype(BF16)
    return high, low


def stack(x):
    high, low = split(x)
    return jnp.concatenate([high, low, high], axis=1)


def matmul(a, b):
    return lax.dot_general(a, b, (((1,), (0,)), ((), ())), preferred_element_type=F32)


def matmul_t(a, b):
    return lax.dot_general(a, b, (((1,), (1,)), ((), ())), preferred_element_type=F32)


def body(
    kern_hbm, vec_hbm, noise_hbm, group_hbm, corr_hbm, stiff_hbm, coup_hbm, nbr_hbm, fwd_hbm, inv_hbm,
    out_ref,
    kern, vec, corr, stiff, coup, nbr, fwd, inv, noise, group, lhs, mix,
    kh, km, vh, ph, part, rs_in, zsum, z_in, mine, resid, rh, grad_a, grad_b, prior,
    halo_lo, halo_hi, line_out, line_in, aid, aid_out,
    load_sem, halo_send, halo_recv, rs_send, rs_recv, tell_send, tell_recv, z_send, z_recv, ag_send, ag_recv,
    share_send, share_recv, line_send, line_recv, aid_recv,
):
    pts, sens = lax.axis_index("pts"), lax.axis_index("sens")
    x, zh, y = pts % 4, pts // 4 % 2, pts // 8
    zl, core = sens // 2, sens % 2

    def plane(dx, dy):
        tx, ty = (x + dx) % 4, (y + dy) % 4
        return ty * 4 + tx, (ty * 2 + zh) * 4 + tx

    own_chunk = y * 4 + x
    z_peer = (y * 2 + 1 - zh) * 4 + x
    up, down = (pts + 1) % 32, (pts + 31) % 32
    core_peer = zl * 2 + 1 - core
    grads = (grad_a, grad_b)
    is0, is3 = (3 - zl) // 3, zl // 3
    is1 = zl % 2 - is3
    is2 = 1 - is0 - is1 - is3
    inner = is1 + is2
    order = [3 * is0 + is2, 2 * is0 + 2 * is1 + 3 * is2 + 2 * is3, is0 + 3 * is1 + is3, zl]
    heads = [is0 + is2 + 2 * is3, order[1], order[2]]

    loads = [
        pltpu.make_async_copy(src, dst, load_sem.at[i])
        for i, (src, dst) in enumerate(
            [
                (kern_hbm, kern), (fwd_hbm.at[0], fwd.at[0]), (vec_hbm, vec),
                (fwd_hbm.at[pl.ds(1, 2)], fwd.at[pl.ds(1, 2)]), (inv_hbm, inv), (corr_hbm, corr),
                (stiff_hbm, stiff), (coup_hbm, coup), (nbr_hbm, nbr), (noise_hbm, noise.at[0]), (group_hbm, group.at[0]),
            ]
        )
    ]
    for i in range(4):
        loads[i].start()

    barrier = pltpu.get_barrier_semaphore()
    greet = [{"pts": plane(dx, dy)[1]} for dx, dy in PLANE]
    greet += [{"pts": plane(dx, dy)[1], "sens": core_peer} for dx, dy in PLANE]
    greet += [{"pts": z_peer}, {"pts": up}, {"pts": down}, {"sens": core_peer}]
    greet += [{"sens": (zl + i) % 4 * 2 + c} for i in range(1, 4) for c in (core, 1 - core)]
    for target in greet:
        pl.semaphore_signal(barrier, inc=1, device_id=target, device_id_type=pl.DeviceIdType.MESH)

    def remote(src, dst, send, recv, target):
        return pltpu.make_async_remote_copy(
            src_ref=src, dst_ref=dst, send_sem=send, recv_sem=recv,
            device_id=target, device_id_type=pl.DeviceIdType.MESH,
        )

    freq = lax.broadcasted_iota(jnp.int32, (1, F2), 1)
    weight = jnp.where(freq * (freq - LANES) == 0, 1.0 / F2, 2.0 / F2).astype(F32)

    lane = lax.broadcasted_iota(jnp.int32, (8, LANES), 1)

    def columns(ft):
        return slice(ft * 2 * LANES, (ft + 1) * 2 * LANES)

    def parts(ft):
        return slice(ft * 2 * LANES, ft * 2 * LANES + LANES), slice(ft * 2 * LANES + LANES, (ft + 1) * 2 * LANES)

    def forward(ft):
        return jnp.concatenate([fwd[ft, 0], fwd[ft, 0], fwd[ft, 1]], axis=0)

    def inverse(v, ft):
        return matmul(stack(v), jnp.concatenate([inv[ft, 0], inv[ft, 0], inv[ft, 1]], axis=0))

    def keep(ft, v, other):
        return jnp.where(lane > 0, v, other) if ft == 0 else v

    def hats(ft, i):
        which, first = i // 2, i % 2 * 4
        rows = slice(first * PD, (first + 4) * PD)
        a = jnp.concatenate([lhs[which, rows], lhs[which, rows, :NT]], axis=1)
        block = columns(ft)
        hat = matmul(a, forward(ft))
        if which == 0:
            hat = hat * weight[:, block]
            kh[first : first + 4, :, block] = hat.reshape(4, PD, 2 * LANES)
            km[first : first + 4, :, ft * LANES : (ft + 1) * LANES] = (hat[:, :LANES] - hat[:, LANES:]).reshape(4, PD, LANES)
        else:
            vh[first : first + 4, :, block] = hat.reshape(4, PD, 2 * LANES)

    def product(ft, i):
        re, im = parts(ft)
        s0 = 2 * i
        acc = [[None] * K for _ in range(6)]
        for p in range(PD // 8):
            rows = pl.ds(p * 8, 8)
            right = []
            for j in range(2):
                c, d = kh[s0 + j, rows, re], kh[s0 + j, rows, im]
                right.append((c, d, c + d))
            for k in range(K):
                a, b = vh[VECTORS[k], rows, re], vh[VECTORS[k], rows, im]
                left = (a, b, a + b)
                for j in range(2):
                    for q in range(3):
                        term = left[q] * right[j][q]
                        old = acc[j * 3 + q][k]
                        acc[j * 3 + q][k] = term if old is None else old + term
        for j in range(2):
            p1, p2, p3 = (
                jnp.concatenate([jnp.sum(v, axis=0, keepdims=True) for v in acc[j * 3 + q]], axis=0)
                for q in range(3)
            )
            rows = pl.ds((s0 + j) * 8, 8)
            ph[rows, re] = keep(ft, p1 - p2, p1)
            ph[rows, im] = keep(ft, p3 - p1 - p2, p2)

    def halve(which, first, rows):
        high, low = split(rows.reshape(-1, NT))
        lhs[which, first : first + high.shape[0], :NT] = high
        lhs[which, first : first + high.shape[0], NT:] = low

    with phase("p_load"):
        loads[0].wait()
        halve(0, 0, kern[...])
        loads[1].wait()
    with phase("p_front0"):
        for i in range(2):
            hats(0, i)
        loads[2].wait()
        loads[3].wait()
        for i in range(4, 11):
            loads[i].start()
        halve(1, 0, vec[...])
        for i in range(2, 4):
            hats(0, i)
    with phase("p_front1"):
        for i in range(4):
            hats(1, i)
            product(0, i)
    with phase("p_front2"):
        for i in range(4):
            hats(2, i)
            product(1, i)
        loads[4].wait()
    with phase("p_front3"):
        for i in range(4):
            product(2, i)
    with phase("p_inv"):
        pred = inverse(ph[:, columns(0)], 0) + inverse(ph[:, columns(1)], 1) + inverse(ph[:, columns(2)], 2)
        part[...] = pred.reshape(SD, K, NT)

    with phase("p_bar"):
        pl.semaphore_wait(barrier, len(greet))

    place = own_chunk
    theirs = place // SD
    rs, others = [], []
    distant = 1 - (y - 2 * core + 5) % 4 // 2
    for i, (dx, near) in enumerate(RS_ORDER):
        row, column = distant + near * (1 - 2 * distant), (x + dx) % 4
        s = row * 4 + column
        owner = core * SD + s
        target = {"pts": ((core * 2 + row) * 2 + zh) * 4 + column, "sens": zl * 2}
        rs.append(remote(part.at[s], rs_in.at[place], rs_send, rs_recv, target))
        others.append(core + (owner - place) * (owner - place) > 0)
        pl.when(others[i])(rs[i].start)

    halo = [
        remote(vec.at[sens, pl.ds(PD - COLS, COLS)], halo_lo, halo_send.at[0], halo_recv.at[0], {"pts": up}),
        remote(vec.at[sens, pl.ds(0, COLS)], halo_hi, halo_send.at[1], halo_recv.at[1], {"pts": down}),
    ]
    share = remote(kh.at[pl.ds(0, SD)], kh.at[pl.ds(SD, SD)], share_send, share_recv, {"sens": core_peer})
    for i in range(5, 11):
        loads[i].wait()
    tell = [
        remote(noise.at[0], noise.at[1], tell_send.at[0], tell_recv.at[0], {"sens": core_peer}),
        remote(group.at[0], group.at[1], tell_send.at[1], tell_recv.at[1], {"sens": core_peer}),
    ]
    for copy in tell + halo + [share]:
        copy.start()
    for copy in tell:
        copy.wait_recv()

    swap = remote(zsum, z_in, z_send, z_recv, {"pts": z_peer})
    ag = []
    for h in (0, 1):
        home = resid.at[place % SD + SD * ((theirs + h) % 2)]
        for i, (dx, dy) in enumerate(PLANE):
            target = {"pts": plane(dx, dy)[1], "sens": zl * 2 + h}
            ag.append(remote(mine.at[h], home, ag_send.at[h], ag_recv, target))
        if h:
            ag.append(remote(mine.at[1], home, ag_send.at[1], ag_recv, {"sens": core_peer}))

    @pl.when(core == 0)
    def _():
        seat = lax.broadcasted_iota(jnp.int32, (1, SD), 1) == place % SD
        scale = jnp.sum(jnp.where(seat, jnp.where(theirs == 0, noise[0], noise[1]), 0.0), axis=1, keepdims=True)
        kind = jnp.sum(jnp.where(seat, jnp.where(theirs == 0, group[0], group[1]), 0), axis=1, keepdims=True)
        matrix = corr[0]
        for g in range(1, NB):
            matrix = jnp.where(kind == g, corr[g], matrix)
        mix_high, mix_low = split(matrix)
        mix[:, :NT] = mix_high
        mix[:, NT : 2 * NT] = mix_high
        mix[:, 2 * NT :] = mix_low

        @pl.when(theirs == 0)
        def _():
            rs_in[place] = part[place % SD]

        with phase("p_rswait"):
            for count in (15, 16):

                @pl.when(theirs == count - 15)
                def _(count=count):
                    rows = rs_in.at[pl.ds(0, count)]
                    remote(rows, rows, rs_send, rs_recv, {"pts": up}).wait_recv()

            total = rs_in[0]
            for i in range(1, 16):
                total = total + rs_in[i]
        zsum[...] = total
        swap.start()
        with phase("p_zwait"):
            swap.wait_recv()
        total = zsum[...] + z_in[...]
        tall = jnp.concatenate([total, jnp.zeros((8, NT), F32)], axis=0)
        value = scale * (total + matmul_t(stack(tall), mix[...])[:K])
        mine[0] = value[:4]
        mine[1] = value[4:]
        for copy in ag:
            copy.start()
        resid[place % SD + SD * theirs] = value[:4]

    with phase("p_prior"):
        for copy in halo:
            copy.wait_recv()
        q = lax.broadcasted_iota(jnp.int32, (PD + 2 * COLS, PD), 0)
        here = lax.broadcasted_iota(jnp.int32, (PD + 2 * COLS, PD), 1) + COLS
        local = nbr[...] - pts * PD + COLS
        links = coup[...]
        diagonal = stiff[...] + jnp.sum(links, axis=0, keepdims=True)
        pick = jnp.where(q == here, diagonal, 0.0)
        for j in range(4):
            pick = pick - jnp.where(q == local[j : j + 1], links[j : j + 1], 0.0)
        padded = jnp.concatenate([halo_lo[...], vec[sens], halo_hi[...]], axis=0)
        term = lax.dot_general(
            pick, padded, (((0,), (0,)), ((), ())),
            precision=lax.Precision.HIGHEST, preferred_element_type=F32,
        )
        for c in range(FT):
            prior[c] = term[:, c * LANES : (c + 1) * LANES]

    with phase("p_share"):
        share.wait_recv()
        for s in range(SD, 2 * SD):
            for ft in range(FT):
                re, im = parts(ft)
                km[s, :, ft * LANES : (ft + 1) * LANES] = kh[s, :, re] - kh[s, :, im]

    with phase("p_agwait"):
        for count in (15, 16):

            @pl.when(core == count - 15)
            def _(count=count):
                rows = resid.at[pl.ds(0, count)]
                remote(rows, rows, ag_send.at[0], ag_recv, {"sens": core_peer}).wait_recv()

    def line_copy(i, j):
        seat, arrival, to = zl, zl, core
        if i == 0:
            seat = inner * zl + (1 - inner) * (4 + core)
            arrival = inner * zl + (1 - inner) * (4 + core * FT + j)
            to = core * inner
        return remote(
            line_out.at[i, j], line_in.at[seat, j], line_send.at[i], line_recv.at[arrival], {"sens": heads[i] * 2 + to}
        )

    assist = remote(line_out.at[2], aid, line_send.at[2], aid_recv, {"sens": core_peer})

    def line_arrival(i):
        return remote(line_in.at[i], line_in.at[i], line_send.at[0], line_recv.at[i], {"sens": core_peer})

    def adjoint(i, ft):
        v, into = order[i], grads[i % 2]
        re, im = parts(ft)
        acc = [None] * (PD // 8)
        for s in range(2 * SD):
            a = rh[2 * ft, pl.ds(s * 4 + v, 8, stride=0), :]
            b = rh[2 * ft + 1, pl.ds(s * 4 + v, 8, stride=0), :]
            ab = a + b
            for p in range(PD // 8):
                rows = pl.ds(p * 8, 8)
                terms = (a * kh[s, rows, re], b * kh[s, rows, im], ab * km[s, rows, ft * LANES : (ft + 1) * LANES])
                acc[p] = terms if s == 0 else tuple(m + n for m, n in zip(acc[p], terms, strict=True))
        for p in range(PD // 8):
            p1, p2, p3 = acc[p]
            into[pl.ds(p * 8, 8), re] = keep(ft, p1 + p2, p1)
            into[pl.ds(p * 8, 8), im] = keep(ft, p3 - p1 + p2, p2)

    def invert(i, ft):
        return inverse(grads[i % 2][:, columns(ft)], ft)

    for i in range(4):
        with phase("p_adj%d" % i):
            if i == 0:
                rows = stack(jnp.concatenate([resid[c] for c in range(2 * SD)], axis=0))

                def spectrum(ft):
                    hat = matmul(rows, forward(ft))
                    rh[2 * ft, : SD * K] = hat[:, :LANES]
                    rh[2 * ft + 1, : SD * K] = hat[:, LANES:]

                spectrum(0)
                spectrum(1)
            adjoint(i, 0)
            if i == 0:
                spectrum(2)
            adjoint(i, 1)
            data = invert(i, 0)
            adjoint(i, 2)
            data = data + invert(i, 1)
            data = data + invert(i, 2)
            for c in range(FT):
                line_out[i, c] = data[:, c * LANES : (c + 1) * LANES]

        for when, which in TURNS[i]:

            @pl.when(core == when)
            def _(which=which):
                for j in range(FT):
                    line_copy(which, j).start()

        if i == 2:

            @pl.when(core * inner == 1)
            def _():
                assist.start()

        if i == 3:

            @pl.when(inner == 0)
            def _():
                for j in range(FT):
                    line_copy(2, j).start()

    with phase("p_relay"):

        @pl.when((1 - core) * inner == 1)
        def _():
            assist.wait_recv()
            for c in (1, 0):
                for j in range(FT):
                    mine_out = aid_out.at[j] if c else line_out.at[2, j]
                    came = line_in.at[4 + c, j]
                    remote(came, came, line_send.at[0], line_recv.at[4 + c * FT + j], {"sens": core_peer}).wait_recv()
                    mine_out[...] = came[...] + (aid[j] if c else line_out[2, j])
                    remote(
                        mine_out, line_in.at[zl, j], line_send.at[2 + c], line_recv.at[zl], {"sens": heads[2] * 2 + c}
                    ).start()

    prior[...] = prior[...] + line_out[3]

    with phase("p_linewait"):

        @pl.when(inner == 1)
        def _():
            for i in (0, 3):
                line_arrival(i).wait_recv()
            prior[...] = prior[...] + line_in[0] + line_in[3]
            line_arrival(3 - zl).wait_recv()
            for c in range(FT):
                out_ref[0, :, c * LANES : (c + 1) * LANES] = prior[c] + line_in[3 - zl, c]

        @pl.when(inner == 0)
        def _():
            for i in (1, 2):
                line_arrival(i).wait_recv()
            for c in range(FT):
                out_ref[0, :, c * LANES : (c + 1) * LANES] = prior[c] + line_in[1, c] + line_in[2, c]

    with phase("p_sends"):
        for copy in halo + tell + [share]:
            copy.wait_send()
        for i in range(3):
            remote(line_out.at[i], line_out.at[i], line_send.at[i], line_recv.at[0], {"sens": core_peer}).wait_send()
        for count in (7, 8):

            @pl.when((core + theirs > 0) == (count == 8))
            def _(count=count):
                rows = part.at[pl.ds(0, count)]
                remote(rows, rows, rs_send, rs_recv, {"pts": up}).wait_send()

        @pl.when(core == 0)
        def _():
            swap.wait_send()

            @pl.when(inner == 1)
            def _():
                remote(aid_out, aid_out, line_send.at[3], line_recv.at[0], {"sens": core_peer}).wait_send()

            for h in range(2):
                rows = resid.at[pl.ds(0, 15 + h)]
                remote(rows, rows, ag_send.at[h], ag_recv, {"sens": core_peer}).wait_send()


def local(kernel, vectors, noise_scale, sensor_group, correlation, stiffness, couplings, neighbors):
    ahead, back = table()
    anywhere = pl.BlockSpec(memory_space=pl.ANY)
    dma = pltpu.SemaphoreType.DMA
    return pl.pallas_call(
        body,
        out_shape=pltpu.VMEM((1, PD, NT), F32),
        in_specs=[anywhere] * 10,
        out_specs=pl.BlockSpec(memory_space=pltpu.VMEM),
        scratch_shapes=[
            pltpu.VMEM((SD, PD, NT), F32),
            pltpu.VMEM((K, PD, NT), F32),
            pltpu.VMEM((NB, NT, NT), F32),
            pltpu.VMEM((1, PD), F32),
            pltpu.VMEM((4, PD), F32),
            pltpu.VMEM((4, PD), jnp.int32),
            pltpu.VMEM((FT, 2, NT, 2 * LANES), BF16),
            pltpu.VMEM((FT, 2, 2 * LANES, NT), BF16),
            pltpu.VMEM((2, 1, SD), F32),
            pltpu.VMEM((2, 1, SD), jnp.int32),
            pltpu.VMEM((2, SD * PD, 2 * NT), BF16),
            pltpu.VMEM((NT, 3 * NT), BF16),
            pltpu.VMEM((2 * SD, PD, F2), F32),
            pltpu.VMEM((2 * SD, PD, NT), F32),
            pltpu.VMEM((K, PD, F2), F32),
            pltpu.VMEM((SD * K, F2), F32),
            pltpu.VMEM((SD, K, NT), F32),
            pltpu.VMEM((16, K, NT), F32),
            pltpu.VMEM((K, NT), F32),
            pltpu.VMEM((K, NT), F32),
            pltpu.VMEM((2, 4, NT), F32),
            pltpu.VMEM((16, 4, NT), F32),
            pltpu.VMEM((2 * FT, SD * K + 8, LANES), F32),
            pltpu.VMEM((PD, F2), F32),
            pltpu.VMEM((PD, F2), F32),
            pltpu.VMEM((FT, PD, LANES), F32),
            pltpu.VMEM((COLS, NT), F32),
            pltpu.VMEM((COLS, NT), F32),
            pltpu.VMEM((4, FT, PD, LANES), F32),
            pltpu.VMEM((6, FT, PD, LANES), F32),
            pltpu.VMEM((FT, PD, LANES), F32),
            pltpu.VMEM((FT, PD, LANES), F32),
            dma((11,)),
            dma((2,)), dma((2,)),
            dma, dma,
            dma((2,)), dma((2,)),
            dma, dma,
            dma((2,)), dma,
            dma, dma,
            dma((4,)), dma((4 + 2 * FT,)), dma,
        ],
        compiler_params=pltpu.CompilerParams(collective_id=0, has_side_effects=True),
    )(
        kernel, vectors, noise_scale.reshape(1, SD), sensor_group.reshape(1, SD), correlation, stiffness.reshape(1, PD),
        couplings, neighbors, jnp.asarray(ahead), jnp.asarray(back),
    )


def solution(mesh):
    in_specs = (
        P("sens", "pts", None),
        P(None, "pts", None),
        P("sens"),
        P("sens"),
        P(),
        P("pts"),
        P(None, "pts"),
        P(None, "pts"),
    )
    return jax.shard_map(
        local, mesh=mesh, in_specs=in_specs, out_specs=P("sens", "pts", None), check_vma=False
    )
```
